32 devices in a mesh: groups: 2 (over y), wloop: 4 (over z), items: 4 (over x, core).
Axes of the slice: x: 2, y: 2, z: 4, core: 2. Of those that a mesh axis runs over, the one named last changes fastest.
Arguments:
- features: bfloat16 [2048, 16384], P(('groups', 'items'), 'wloop'), parts along dimension 0, may hold values from -6 to 6
- cotangent: bfloat16 [2048, 16384], P(('groups', 'items'), 'wloop'), parts along dimension 0, may hold values from -6 to 6
- block_weights: bfloat16 [256, 256, 256], P('wloop'), may hold values from -0.1875 to 0.1875
- block_rows: int32 [256], P('wloop'), may hold values from 0 to 63, as said below
- block_cols: int32 [256], P('wloop'), may hold values from 0 to 63, as said below
- lowrank_in: bfloat16 [128, 16384], P(None, 'wloop'), may hold values from -0.046875 to 0.046875
- lowrank_out: bfloat16 [128, 16384], P(None, 'wloop'), may hold values from -0.5 to 0.5
Outputs:
- mixed: bfloat16 [2048, 16384], P(('groups', 'items'), 'wloop'), parts along dimension 0
- block_grads: float32 [512, 256, 256], P(('groups', 'items'), 'wloop'), parts along dimension 0
- grad_in: float32 [256, 16384], P(('groups', 'items'), 'wloop'), parts along dimension 0
- grad_out: float32 [256, 16384], P(('groups', 'items'), 'wloop'), parts along dimension 0
The draws below stay inside these ranges and needn't reach their ends.
There are 2 independent parts, one for each index of `groups`. The reference program is written for one: setup_inputs(seed, part) draws one part's arguments, and reference() takes and returns one part's arrays. A program takes and returns all parts, laid end to end along the dimension named above; an argument that names none is the same for every part. Nothing has to cross between parts.
Inputs may be any that keep to these rules, and one draw needn't show every extreme that they name: `block_rows`: the stored blocks form a strided block pattern: every input block column c appears in exactly 4 stored blocks, whose output blocks are c, c xor 1, c xor (16) and c xor (32); the stored blocks on one index of wloop are exactly those of its 16 input block columns, in an order drawn afresh. `block_cols`: the input block column of each stored block, as described for block_rows; the stored blocks on one index of wloop have input columns within that index's range of 16 columns.
All inputs are finite; a program needn't handle non-finite values.
Results may differ from the reference program's by a relative error of at most 0.0039.
Values may be sent and summed in bfloat16 or wider, within the bound.
No kernel may reach another device: no remote copies, remote signals or barrier semaphores. Data moves between devices by JAX's collectives and lax.ppermute only.
A program may use at most 128 MiB of HBM per device.

```python
import jax
import jax.numpy as jnp
from jax import lax

WIDTH = 16384
BLOCK = 256
LOWRANK = 128
PER_COLUMN = 4
ITEMS = 1024
STORED = 256
N_WLOOP = 4


def pattern_lists(key):
    count = WIDTH // BLOCK
    share = count // N_WLOOP
    local = PER_COLUMN * share
    keys = jax.random.split(jax.random.fold_in(key, 7), N_WLOOP)
    orders = jax.vmap(lambda one: jax.random.permutation(one, local))(keys).astype(jnp.int32)
    device = jnp.arange(N_WLOOP, dtype=jnp.int32)[:, None]
    columns = device * share + orders // PER_COLUMN
    table = jnp.array([0, 1, count // 4, count // 2], jnp.int32)
    strides = table[orders % PER_COLUMN]
    outputs = jnp.bitwise_xor(columns, strides)
    return (outputs.reshape(-1).astype(jnp.int32), columns.reshape(-1).astype(jnp.int32))


def draw_block_rows(key, part):
    return pattern_lists(key)[0]


def draw_block_cols(key, part):
    return pattern_lists(key)[1]


def shard_levels(stream_key, dims, cuts, least, largest):
    def one(dim, blocks):
        draws = jax.random.uniform(jax.random.fold_in(jax.random.fold_in(stream_key, 6), dim), (blocks,), jnp.float32, least / len(cuts), largest / len(cuts))
        return jnp.repeat(jnp.exp(draws), dims[dim] // blocks).reshape((-1,) + (1,) * (len(dims) - dim - 1))

    loudness = one(*cuts[0])
    for cut in cuts[1:]:
        loudness = loudness * one(*cut)
    return loudness


def centred(own_key, extent, scale, limit, cuts=(), held_as=jnp.bfloat16):
    result = scale * jax.random.normal(own_key, extent, jnp.float32)
    if cuts:
        result = result * shard_levels(own_key, extent, cuts, -0.22, 0.18)
    return jnp.clip(result, -limit, limit).astype(held_as)


def setup_inputs(seed: int = 0, part: int = 0) -> dict:
    splits = jax.random.split(jax.random.key(seed), 8)
    part_keys = jax.random.split(jax.random.fold_in(splits[7], part), 8)
    features = centred(part_keys[0], (ITEMS, WIDTH), 1.0, 6.0, ((0, 4), (1, 4)))
    cotangent = centred(part_keys[1], (ITEMS, WIDTH), 1.0, 6.0, ((0, 4), (1, 4)))
    block_weights = centred(splits[2], (STORED, BLOCK, BLOCK), (PER_COLUMN * BLOCK) ** -0.5, 0.1875, ((0, 4),))
    block_rows = draw_block_rows(jax.random.fold_in(splits[7], 71), part)
    block_cols = draw_block_cols(jax.random.fold_in(splits[7], 71), part)
    lowrank_in = centred(splits[5], (LOWRANK, WIDTH), WIDTH ** -0.5, 0.046875, ((1, 4),))
    lowrank_out = centred(splits[6], (LOWRANK, WIDTH), LOWRANK ** -0.5, 0.5, ((1, 4),))
    return {"features": features, "cotangent": cotangent, "block_weights": block_weights, "block_rows": block_rows, "block_cols": block_cols, "lowrank_in": lowrank_in, "lowrank_out": lowrank_out}


def reference(features, cotangent, block_weights, block_rows, block_cols, lowrank_in, lowrank_out):
    def step(total, inputs):
        weight, row, col = inputs
        start_in = (col * BLOCK).astype(jnp.int32)
        start_out = (row * BLOCK).astype(jnp.int32)
        taken = lax.dynamic_slice_in_dim(features, start_in, BLOCK, 1)
        grads = lax.dynamic_slice_in_dim(cotangent, start_out, BLOCK, 1)
        contrib = jnp.dot(taken, weight.T, preferred_element_type=jnp.float32)
        current = lax.dynamic_slice_in_dim(total, start_out, BLOCK, 1)
        total = lax.dynamic_update_slice_in_dim(total, current + contrib, start_out, 1)
        grad = jnp.dot(grads.T, taken, preferred_element_type=jnp.float32)
        return total, grad

    start = jnp.zeros((features.shape[0], WIDTH), jnp.float32)
    sparse, grads = lax.scan(step, start, (block_weights, block_rows.astype(jnp.int32), block_cols.astype(jnp.int32)))
    codes = jnp.dot(features, lowrank_in.T, preferred_element_type=jnp.float32).astype(jnp.bfloat16)
    backs = jnp.dot(cotangent, lowrank_out.T, preferred_element_type=jnp.float32).astype(jnp.bfloat16)
    mixed = (sparse + jnp.dot(codes, lowrank_out, preferred_element_type=jnp.float32)).astype(jnp.bfloat16)
    block_grads = jnp.transpose(grads, (1, 0, 2))
    grad_in = jnp.dot(backs.T, features, preferred_element_type=jnp.float32)
    grad_out = jnp.dot(codes.T, cotangent, preferred_element_type=jnp.float32)
    return mixed, block_grads, grad_in, grad_out
```

```python
import functools

import jax
import jax.numpy as jnp
from jax import lax
from jax.experimental import pallas as pl
from jax.experimental.pallas import tpu as pltpu
from jax.sharding import PartitionSpec as P

WIDTH = 16384
BLOCK = 256
CHUNKS = 4


F32 = jnp.float32
BF16 = jnp.bfloat16


def swapped(block, axis, apart):
    count = lax.axis_size(axis)
    return lax.ppermute(block, axis, [(one, one ^ (1 << apart)) for one in range(count)])


def after(value, *deps):
    return lax.optimization_barrier((value, *deps))[0]


def pick(values, index, dim):
    return lax.dynamic_index_in_dim(values, index, dim, keepdims=False)


def grad_body(pairs, part, bit_ref, g_ref, *refs):
    f_refs, (send_ref, keep_ref, acc_ref) = refs[:-3], refs[-3:]
    bit = bit_ref[0]
    blocks = g_ref.shape[1] // BLOCK
    halves = send_ref.shape[2]
    for at in range(blocks):
        for slot, (f_at, flip) in enumerate(pairs):
            g_at = at ^ flip
            acc_ref[...] = lax.dot_general(
                g_ref[:, g_at * BLOCK : (g_at + 1) * BLOCK],
                f_refs[f_at][:, at * BLOCK : (at + 1) * BLOCK],
                (((0,), (0,)), ((), ())),
                preferred_element_type=F32,
            )
            for half in range(halves):
                first = pl.multiple_of((2 * half + bit) * part, part)
                other = pl.multiple_of((2 * half + 1 - bit) * part, part)
                keep_ref[slot, at, half] = acc_ref[pl.ds(first, part), :]
                send_ref[slot, at, half] = acc_ref[pl.ds(other, part), :].astype(BF16)


def pair_grads(bit, cotangent, features, pairs, first, count, parts):
    rows_here = cotangent.shape[0]
    part = BLOCK // parts
    step = min(4, count)
    shape = (2, count, parts // 2, part, BLOCK)
    block = (2, step, parts // 2, part, BLOCK)
    out_spec = pl.BlockSpec(block, lambda at, bit_ref: (0, at, 0, 0, 0))
    skip = first // step
    return pl.pallas_call(
        functools.partial(grad_body, pairs, part),
        grid_spec=pltpu.PrefetchScalarGridSpec(
            num_scalar_prefetch=1,
            grid=(count // step,),
            in_specs=[pl.BlockSpec((rows_here, step * BLOCK), lambda at, bit_ref: (0, at + skip))]
            + [pl.BlockSpec((rows_here, step * BLOCK), lambda at, bit_ref: (0, at))] * len(features),
            out_specs=(out_spec, out_spec),
            scratch_shapes=[pltpu.VMEM((BLOCK, BLOCK), F32)],
        ),
        out_shape=(jax.ShapeDtypeStruct(shape, BF16), jax.ShapeDtypeStruct(shape, F32)),
        cost_estimate=pl.CostEstimate(
            flops=4 * count * rows_here * BLOCK * BLOCK,
            bytes_accessed=count * BLOCK * (2 * rows_here * 3 + 6 * BLOCK),
            transcendentals=0,
        ),
        name="pair_grads",
    )(bit, cotangent, *features)


def items_sum(send, keep, index, dim):
    bits = lax.axis_size("items").bit_length() - 1
    total = keep + swapped(send, "items", 0).astype(F32)
    for level in range(1, bits):
        mine = (index >> level) & 1
        shape = total.shape
        split = total.reshape(*shape[:dim], shape[dim] // 2, 2, *shape[dim + 1 :])
        total = pick(split, mine, dim + 1) + swapped(
            pick(split, 1 - mine, dim + 1).astype(BF16), "items", level
        ).astype(F32)
    return total.reshape(*total.shape[:dim], *total.shape[dim + 1 :])


def copy_body(where_ref, in_ref, out_ref):
    out_ref[...] = in_ref[...]


def weight_share(block_weights, where, unit, count):
    def source(index, where_ref):
        return where_ref[2 * index], where_ref[2 * index + 1], 0

    return pl.pallas_call(
        copy_body,
        grid_spec=pltpu.PrefetchScalarGridSpec(
            num_scalar_prefetch=1,
            grid=(2 * count,),
            in_specs=[pl.BlockSpec((1, unit, BLOCK), source)],
            out_specs=pl.BlockSpec((1, unit, BLOCK), lambda index, where_ref: (index, 0, 0)),
        ),
        out_shape=jax.ShapeDtypeStruct((2 * count, unit, BLOCK), BF16),
        cost_estimate=pl.CostEstimate(
            flops=0, bytes_accessed=8 * count * unit * BLOCK, transcendentals=0
        ),
        name="weight_share",
    )(where, block_weights)


def mixed_body(share, chunks, pieces, pos_ref, loc_ref, *refs):
    own_ref, flip_ref, w0_ref, w1_ref, codes_ref, low_ref = refs[:6]
    far_refs = refs[6 : 6 + 2 * chunks]
    w_refs = refs[6 + 2 * chunks : 6 + 2 * chunks + 2 * pieces]
    out_ref, acc_ref = refs[-2:]
    dims = (((1,), (1,)), ((), ()))
    at = pl.program_id(0)
    total = lax.dot_general(own_ref[...], w0_ref[0], dims, preferred_element_type=F32)
    total += lax.dot_general(flip_ref[...], w1_ref[0], dims, preferred_element_type=F32)
    total += jnp.dot(codes_ref[...], low_ref[...], preferred_element_type=F32)
    acc_ref[...] = total
    per = share // chunks
    for chunk in range(chunks):

        @pl.when(at // per == chunk)
        def _(chunk=chunk):
            extra = acc_ref[...]
            for far in range(2):
                weight = jnp.concatenate(
                    [w_refs[far * pieces + piece][0] for piece in range(pieces)], axis=0
                )
                extra += lax.dot_general(
                    far_refs[far * chunks + chunk][...], weight, dims, preferred_element_type=F32
                )
            out_ref[...] = extra.astype(BF16)


def mixed_kernel(features, block_weights, codes, lowrank_out, far, far_weights, pos, loc):
    rows_here, width = features.shape
    share = width // BLOCK
    chunks = len(far[0])
    per = share // chunks
    unit = far_weights[0].shape[1]
    pieces = BLOCK // unit

    def far_map(chunk):
        return lambda at, pos_ref, loc_ref: (0, jnp.clip(at - chunk * per, 0, per - 1))

    def weight_map(piece):
        return lambda at, pos_ref, loc_ref: (loc_ref[at * pieces + piece], 0, 0)

    tall = (rows_here, BLOCK)
    in_specs = [
        pl.BlockSpec(tall, lambda at, pos_ref, loc_ref: (0, at)),
        pl.BlockSpec(tall, lambda at, pos_ref, loc_ref: (0, at ^ 1)),
        pl.BlockSpec((1, BLOCK, BLOCK), lambda at, pos_ref, loc_ref: (pos_ref[at], 0, 0)),
        pl.BlockSpec(
            (1, BLOCK, BLOCK), lambda at, pos_ref, loc_ref: (pos_ref[share + (at ^ 1)], 0, 0)
        ),
        pl.BlockSpec(codes.shape, lambda at, pos_ref, loc_ref: (0, 0)),
        pl.BlockSpec((lowrank_out.shape[0], BLOCK), lambda at, pos_ref, loc_ref: (0, at)),
    ]
    in_specs += [pl.BlockSpec(tall, far_map(chunk)) for _ in range(2) for chunk in range(chunks)]
    in_specs += [
        pl.BlockSpec((1, unit, BLOCK), weight_map(piece)) for _ in range(2) for piece in range(pieces)
    ]
    weights = [far_weights[way] for way in range(2) for _ in range(pieces)]
    return pl.pallas_call(
        functools.partial(mixed_body, share, chunks, pieces),
        grid_spec=pltpu.PrefetchScalarGridSpec(
            num_scalar_prefetch=2,
            grid=(share,),
            in_specs=in_specs,
            out_specs=pl.BlockSpec(tall, lambda at, pos_ref, loc_ref: (0, at)),
            scratch_shapes=[pltpu.VMEM(tall, F32)],
        ),
        out_shape=jax.ShapeDtypeStruct((rows_here, width), BF16),
        cost_estimate=pl.CostEstimate(
            flops=9 * share * rows_here * BLOCK * BLOCK,
            bytes_accessed=share * BLOCK * 2 * (4 * rows_here + 4 * BLOCK),
            transcendentals=0,
        ),
        name="mixed",
    )(pos, loc, features, features, block_weights, block_weights, codes, lowrank_out, *far[0], *far[1], *weights)


def place_body(share, chunks, pos_ref, own_ref, *refs):
    far_refs, out_ref = refs[:-1], refs[-1]
    rows = own_ref.shape[2]
    stored = 4 * share
    per = share // chunks
    for way in range(4):
        for at in range(share):
            if way < 2:
                block = own_ref[way, at]
            else:
                block = far_refs[(way - 2) * chunks + at // per][at % per].astype(F32)
            out_ref[:, pos_ref[way * share + at], :] = block


def place_kernel(own, far, pos):
    _, share, part, _ = own.shape
    chunks = len(far[0])
    per = share // chunks
    rows = 16
    far_spec = pl.BlockSpec((per, rows, BLOCK), lambda at, pos_ref: (0, at, 0))
    return pl.pallas_call(
        functools.partial(place_body, share, chunks),
        grid_spec=pltpu.PrefetchScalarGridSpec(
            num_scalar_prefetch=1,
            grid=(part // rows,),
            in_specs=[pl.BlockSpec((2, share, rows, BLOCK), lambda at, pos_ref: (0, 0, at, 0))]
            + [far_spec] * (2 * chunks),
            out_specs=pl.BlockSpec((rows, 4 * share, BLOCK), lambda at, pos_ref: (at, 0, 0)),
        ),
        out_shape=jax.ShapeDtypeStruct((part, 4 * share, BLOCK), F32),
        cost_estimate=pl.CostEstimate(
            flops=0, bytes_accessed=32 * share * part * BLOCK, transcendentals=0
        ),
        name="place",
    )(pos, own, *far[0], *far[1])


def body(features, cotangent, block_weights, block_rows, block_cols, lowrank_in, lowrank_out):
    rows_here, width = features.shape
    share = width // BLOCK
    count = WIDTH // BLOCK
    stored = block_weights.shape[0]
    chunks = min(CHUNKS, share)
    per = share // chunks
    items = lax.axis_size("items")
    item = lax.axis_index("items")
    bits = items.bit_length() - 1
    ways = lax.axis_size("wloop")
    place = lax.axis_index("wloop")
    way_bits = ways.bit_length() - 1
    far_bits = (way_bits - 2, way_bits - 1)
    part = BLOCK // items

    stride_of = jnp.bitwise_xor(block_rows, block_cols)
    stride_table = jnp.array([0, 1, count // 4, count // 2], jnp.int32)
    local_cols = block_cols % share
    key_hit = (stride_of[None, None, :] == stride_table[:, None, None]) & (
        local_cols[None, None, :] == jnp.arange(share, dtype=jnp.int32)[None, :, None]
    )
    pos = jnp.sum(
        jnp.where(key_hit, jnp.arange(stored, dtype=jnp.int32)[None, None, :], 0), axis=2
    ).astype(jnp.int32)
    pos_flat = pos.reshape(-1)

    sent = [features[:, one * per * BLOCK : (one + 1) * per * BLOCK] for one in range(chunks)]
    far = [[swapped(piece, "wloop", bit) for piece in sent] for bit in far_bits]

    unit = min(BLOCK, share * BLOCK // items)
    units = share * BLOCK // items // unit
    pieces = BLOCK // unit
    numbers = item * units + jnp.arange(units, dtype=jnp.int32)
    where = jnp.stack(
        [
            jnp.take(pos[2:], numbers // pieces, axis=1),
            jnp.broadcast_to(numbers % pieces, (2, units)),
        ],
        axis=2,
    ).reshape(-1)
    shares = weight_share(block_weights, where.astype(jnp.int32), unit, units)
    shares = shares.reshape(2, units, unit, BLOCK)
    far_weights = []
    for way in range(2):
        held = swapped(shares[way], "wloop", far_bits[way])
        for level in range(bits - 1, -1, -1):
            held = jnp.concatenate([held, swapped(held, "items", level)], axis=0)
        far_weights.append(held)
    all_numbers = jnp.arange(share * pieces, dtype=jnp.int32)
    apart = (all_numbers // units) ^ item
    slot = jnp.zeros_like(apart)
    for level in range(bits):
        slot = slot * 2 + ((apart >> level) & 1)
    loc = (slot * units + all_numbers % units).astype(jnp.int32)

    dims = (((1,), (1,)), ((), ()))
    codes = jnp.stack(
        [
            lax.dot_general(features, lowrank_in, dims, preferred_element_type=F32),
            lax.dot_general(cotangent, lowrank_out, dims, preferred_element_type=F32),
        ]
    )
    for level in range(way_bits):
        mine = (place >> level) & 1
        split = codes.reshape(2, 2, codes.shape[1] // 2, codes.shape[2])
        codes = pick(split, mine, 1) + swapped(pick(split, 1 - mine, 1), "wloop", level)
    codes = codes.astype(BF16)
    for level in range(way_bits - 1, -1, -1):
        mine = (place >> level) & 1
        other = swapped(codes, "wloop", level)
        codes = jnp.where(
            mine == 0,
            jnp.concatenate([codes, other], axis=1),
            jnp.concatenate([other, codes], axis=1),
        )
    codes, backs = codes[0], codes[1]

    bit = (item & 1).astype(jnp.int32).reshape(1)
    own = items_sum(
        *pair_grads(bit, cotangent, [features], ((0, 0), (0, 1)), 0, share, items), item, 2
    )
    returned = [[], []]
    for one in range(chunks):
        done = items_sum(
            *pair_grads(
                bit,
                cotangent,
                [far[0][one], far[1][one]],
                ((0, 0), (1, 0)),
                one * per,
                per,
                items,
            ),
            item,
            2,
        ).astype(BF16)
        for way in range(2):
            returned[way].append(swapped(done[way], "wloop", far_bits[way]))

    cols_dims = (((0,), (0,)), ((), ()))
    terms = jnp.stack(
        [
            lax.dot_general(backs, features, cols_dims, preferred_element_type=F32),
            lax.dot_general(codes, cotangent, cols_dims, preferred_element_type=F32),
        ]
    ).reshape(2, items // 2, 2, lowrank_in.shape[0] // items, width)
    low_grads = items_sum(
        pick(terms, 1 - bit[0], 2).astype(BF16), pick(terms, bit[0], 2), item, 1
    )

    mixed = mixed_kernel(
        features, block_weights, codes, lowrank_out, far, far_weights, pos_flat, loc
    )
    block_grads = place_kernel(own, returned, pos_flat)
    return (mixed, block_grads, low_grads[0], low_grads[1])


def solution(mesh):
    return jax.shard_map(
        body,
        mesh=mesh,
        in_specs=(
            P(("groups", "items"), "wloop"),
            P(("groups", "items"), "wloop"),
            P("wloop", None, None),
            P("wloop"),
            P("wloop"),
            P(None, "wloop"),
            P(None, "wloop"),
        ),
        out_specs=(
            P(("groups", "items"), "wloop"),
            P(("groups", "items"), "wloop", None),
            P(("groups", "items"), "wloop"),
            P(("groups", "items"), "wloop"),
        ),
        check_vma=False,
    )
```

```python
import functools

import jax
import jax.numpy as jnp
from jax import lax
from jax.experimental import pallas as pl
from jax.experimental.pallas import tpu as pltpu
from jax.sharding import PartitionSpec as P


WIDTH = 16384
BLOCK = 256
CHUNKS = 4


F32 = jnp.float32
BF16 = jnp.bfloat16


def swapped(block, axis, apart):
    count = lax.axis_size(axis)
    return lax.ppermute(block, axis, [(one, one ^ (1 << apart)) for one in range(count)])


def pick(values, index, dim):
    return lax.dynamic_index_in_dim(values, index, dim, keepdims=False)


def grad_body(pairs, part, bit_ref, g_ref, *refs):
    f_refs, (send_ref, keep_ref, acc_ref) = refs[:-3], refs[-3:]
    bit = bit_ref[0]
    blocks = g_ref.shape[1] // BLOCK
    halves = send_ref.shape[0]
    for at in range(blocks):
        for slot, (f_at, flip) in enumerate(pairs):
            g_at = at ^ flip
            acc_ref[...] = lax.dot_general(
                g_ref[:, g_at * BLOCK : (g_at + 1) * BLOCK],
                f_refs[f_at][:, at * BLOCK : (at + 1) * BLOCK],
                (((0,), (0,)), ((), ())),
                preferred_element_type=F32,
            )
            for half in range(halves):
                first = pl.multiple_of((2 * half + bit) * part, part)
                other = pl.multiple_of((2 * half + 1 - bit) * part, part)
                keep_ref[half, slot, at] = acc_ref[pl.ds(first, part), :]
                send_ref[half, slot, at] = acc_ref[pl.ds(other, part), :].astype(BF16)


def pair_grads(bit, cotangent, features, pairs, first, count, parts):
    rows_here = cotangent.shape[0]
    part = BLOCK // parts
    step = min(2, count)
    shape = (parts // 2, 2, count, part, BLOCK)
    block = (parts // 2, 2, step, part, BLOCK)
    out_spec = pl.BlockSpec(block, lambda at, bit_ref: (0, 0, at, 0, 0))
    skip = first // step
    return pl.pallas_call(
        functools.partial(grad_body, pairs, part),
        grid_spec=pltpu.PrefetchScalarGridSpec(
            num_scalar_prefetch=1,
            grid=(count // step,),
            in_specs=[pl.BlockSpec((rows_here, step * BLOCK), lambda at, bit_ref: (0, at + skip))]
            + [pl.BlockSpec((rows_here, step * BLOCK), lambda at, bit_ref: (0, at))] * len(features),
            out_specs=(out_spec, out_spec),
            scratch_shapes=[pltpu.VMEM((BLOCK, BLOCK), F32)],
        ),
        out_shape=(jax.ShapeDtypeStruct(shape, BF16), jax.ShapeDtypeStruct(shape, F32)),
        cost_estimate=pl.CostEstimate(
            flops=4 * count * rows_here * BLOCK * BLOCK,
            bytes_accessed=count * BLOCK * (2 * rows_here * 3 + 6 * BLOCK),
            transcendentals=0,
        ),
        name="pair_grads",
    )(bit, cotangent, *features)


def low_body(part, bit_ref, b_ref, f_ref, c_ref, g_ref, send_ref, keep_ref, acc_ref):
    bit = bit_ref[0]
    for slot, (small, wide) in enumerate(((b_ref, f_ref), (c_ref, g_ref))):
        acc_ref[...] = lax.dot_general(
            small[...], wide[...], (((0,), (0,)), ((), ())), preferred_element_type=F32
        )
        for half in range(send_ref.shape[0]):
            first = pl.multiple_of((2 * half + bit) * part, part)
            other = pl.multiple_of((2 * half + 1 - bit) * part, part)
            keep_ref[half, slot] = acc_ref[pl.ds(first, part), :]
            send_ref[half, slot] = acc_ref[pl.ds(other, part), :].astype(BF16)


def low_kernel(bit, backs, features, codes, cotangent, parts):
    rows_here, width = features.shape
    rank = codes.shape[1]
    part = rank // parts
    step = min(1024, width)
    out_spec = pl.BlockSpec((parts // 2, 2, part, step), lambda at, bit_ref: (0, 0, 0, at))
    shape = (parts // 2, 2, part, width)
    wide = pl.BlockSpec((rows_here, step), lambda at, bit_ref: (0, at))
    small = pl.BlockSpec((rows_here, rank), lambda at, bit_ref: (0, 0))
    return pl.pallas_call(
        functools.partial(low_body, part),
        grid_spec=pltpu.PrefetchScalarGridSpec(
            num_scalar_prefetch=1,
            grid=(width // step,),
            in_specs=[small, wide, small, wide],
            out_specs=(out_spec, out_spec),
            scratch_shapes=[pltpu.VMEM((rank, step), F32)],
        ),
        out_shape=(jax.ShapeDtypeStruct(shape, BF16), jax.ShapeDtypeStruct(shape, F32)),
        cost_estimate=pl.CostEstimate(
            flops=4 * rank * rows_here * width,
            bytes_accessed=width * (4 * rows_here + 6 * rank),
            transcendentals=0,
        ),
        name="low_grads",
    )(bit, backs, features, codes, cotangent)


def items_sum(send, keep, index):
    bits = lax.axis_size("items").bit_length() - 1
    came = swapped(send, "items", 0)
    for level in range(1, bits):
        mine = (index >> level) & 1
        shape = (keep.shape[0] // 2, 2, *keep.shape[1:])
        keep, came = keep.reshape(shape), came.reshape(shape)
        leave = pick(keep, 1 - mine, 1) + pick(came, 1 - mine, 1).astype(F32)
        keep = pick(keep, mine, 1) + pick(came, mine, 1).astype(F32)
        came = swapped(leave.astype(BF16), "items", level)
    return (keep + came.astype(F32))[0]


def share_body(share, units, unit, pos_ref, item_ref, w_ref, out_ref, sems):
    pieces = BLOCK // unit
    copies = []
    for way in range(2):
        for one in range(units):
            number = item_ref[0] * units + one
            block = pos_ref[(2 + way) * share + lax.div(number, pieces)]
            first = pl.multiple_of(lax.rem(number, pieces) * unit, unit)
            copies.append(
                pltpu.make_async_copy(
                    w_ref.at[block, pl.ds(first, unit), :],
                    out_ref.at[way, one],
                    sems.at[way * units + one],
                )
            )
    for copy in copies:
        copy.start()
    for copy in copies:
        copy.wait()


def weight_share(block_weights, pos, item, share, unit, units):
    return pl.pallas_call(
        functools.partial(share_body, share, units, unit),
        in_specs=[
            pl.BlockSpec(memory_space=pltpu.SMEM),
            pl.BlockSpec(memory_space=pltpu.SMEM),
            pl.BlockSpec(memory_space=pl.ANY),
        ],
        out_specs=pl.BlockSpec(memory_space=pltpu.VMEM),
        out_shape=jax.ShapeDtypeStruct((2, units, unit, BLOCK), BF16),
        scratch_shapes=[pltpu.SemaphoreType.DMA((2 * units,))],
        cost_estimate=pl.CostEstimate(
            flops=0, bytes_accessed=8 * units * unit * BLOCK, transcendentals=0
        ),
        name="weight_share",
    )(pos, item, block_weights)


def mixed_body(share, chunks, units, unit, bits, pos_ref, item_ref, f_ref, w_ref, codes_ref, low_ref, *refs):
    far_refs, refs = refs[: 2 * chunks], refs[2 * chunks :]
    far_w, out_ref = refs[:2], refs[2]
    f_buf, low_buf, far_bufs, w_buf, out_buf, in_sems, w_sems, out_sems = (
        refs[3],
        refs[4],
        refs[5],
        refs[6],
        refs[7],
        refs[8],
        refs[9],
        refs[10],
    )
    dims = (((1,), (1,)), ((), ()))
    pieces = BLOCK // unit
    per = share // chunks
    wide = per * BLOCK
    item = item_ref[0]

    def slot_of(number):
        apart = lax.div(number, units) ^ item
        slot = jnp.int32(0)
        for level in range(bits):
            slot = slot * 2 + ((apart >> level) & 1)
        return slot * units + lax.rem(number, units)

    loads, weights = [], []
    for chunk in range(chunks):
        cols = pl.ds(chunk * wide, wide)
        loads.append(
            [
                pltpu.make_async_copy(f_ref.at[:, cols], f_buf.at[:, cols], in_sems.at[chunk, 0]),
                pltpu.make_async_copy(low_ref.at[:, cols], low_buf.at[:, cols], in_sems.at[chunk, 1]),
            ]
            + [
                pltpu.make_async_copy(
                    far_refs[way * chunks + chunk], far_bufs.at[way, chunk], in_sems.at[chunk, 2 + way]
                )
                for way in range(2)
            ]
        )
        chunk_weights = []
        for at in range(chunk * per, (chunk + 1) * per):
            chunk_weights.append(
                pltpu.make_async_copy(w_ref.at[pos_ref[at]], w_buf.at[0, at], w_sems.at[0, at, 0])
            )
            chunk_weights.append(
                pltpu.make_async_copy(
                    w_ref.at[pos_ref[share + (at ^ 1)]], w_buf.at[1, at], w_sems.at[1, at, 0]
                )
            )
            for way in range(2):
                for piece in range(pieces):
                    chunk_weights.append(
                        pltpu.make_async_copy(
                            far_w[way].at[slot_of(jnp.int32(at * pieces + piece))],
                            w_buf.at[2 + way, at, pl.ds(piece * unit, unit), :],
                            w_sems.at[2 + way, at, piece],
                        )
                    )
        weights.append(chunk_weights)
    for chunk in range(chunks):
        for copy in loads[chunk] + weights[chunk]:
            copy.start()
    stores = []
    for chunk in range(chunks):
        for copy in loads[chunk] + weights[chunk]:
            copy.wait()
        for at in range(chunk * per, (chunk + 1) * per):
            own = slice(at * BLOCK, (at + 1) * BLOCK)
            flip = slice((at ^ 1) * BLOCK, ((at ^ 1) + 1) * BLOCK)
            local = slice((at - chunk * per) * BLOCK, (at - chunk * per + 1) * BLOCK)
            total = lax.dot_general(f_buf[:, own], w_buf[0, at], dims, preferred_element_type=F32)
            total += lax.dot_general(f_buf[:, flip], w_buf[1, at], dims, preferred_element_type=F32)
            for way in range(2):
                total += lax.dot_general(
                    far_bufs[way, chunk, :, local],
                    w_buf[2 + way, at],
                    dims,
                    preferred_element_type=F32,
                )
            total += jnp.dot(codes_ref[...], low_buf[:, own], preferred_element_type=F32)
            out_buf[:, own] = total.astype(BF16)
        cols = pl.ds(chunk * wide, wide)
        store = pltpu.make_async_copy(out_buf.at[:, cols], out_ref.at[:, cols], out_sems.at[chunk])
        store.start()
        stores.append(store)
    for store in stores:
        store.wait()


def mixed_kernel(features, block_weights, codes, lowrank_out, far, far_weights, pos, item, units, bits):
    rows_here, width = features.shape
    share = width // BLOCK
    chunks = len(far[0])
    unit = far_weights[0].shape[1]
    hbm = pl.BlockSpec(memory_space=pl.ANY)
    smem = pl.BlockSpec(memory_space=pltpu.SMEM)
    return pl.pallas_call(
        functools.partial(mixed_body, share, chunks, units, unit, bits),
        in_specs=[smem, smem, hbm, hbm, pl.BlockSpec(memory_space=pltpu.VMEM), hbm]
        + [hbm] * (2 * chunks + 2),
        out_specs=hbm,
        out_shape=jax.ShapeDtypeStruct((rows_here, width), BF16),
        scratch_shapes=[
            pltpu.VMEM((rows_here, width), BF16),
            pltpu.VMEM(lowrank_out.shape, BF16),
            pltpu.VMEM((2, chunks, rows_here, width // chunks), BF16),
            pltpu.VMEM((4, share, BLOCK, BLOCK), BF16),
            pltpu.VMEM((rows_here, width), BF16),
            pltpu.SemaphoreType.DMA((chunks, 4)),
            pltpu.SemaphoreType.DMA((4, share, BLOCK // unit)),
            pltpu.SemaphoreType.DMA((chunks,)),
        ],
        cost_estimate=pl.CostEstimate(
            flops=9 * share * rows_here * BLOCK * BLOCK,
            bytes_accessed=share * BLOCK * 2 * (4 * rows_here + 4 * BLOCK),
            transcendentals=0,
        ),
        name="mixed",
    )(pos, item, features, block_weights, codes, lowrank_out, *far[0], *far[1], *far_weights)


def place_body(share, chunks, pos_ref, own_ref, *refs):
    far_refs, out_ref = refs[:-1], refs[-1]
    per = share // chunks
    for way in range(4):
        for at in range(share):
            if way < 2:
                block = own_ref[way, at]
            else:
                block = far_refs[(way - 2) * chunks + at // per][at % per].astype(F32)
            out_ref[:, pos_ref[way * share + at], :] = block


def place_kernel(own, far, pos):
    _, share, part, _ = own.shape
    chunks = len(far[0])
    per = share // chunks
    rows = 16
    far_spec = pl.BlockSpec((per, rows, BLOCK), lambda at, pos_ref: (0, at, 0))
    return pl.pallas_call(
        functools.partial(place_body, share, chunks),
        grid_spec=pltpu.PrefetchScalarGridSpec(
            num_scalar_prefetch=1,
            grid=(part // rows,),
            in_specs=[pl.BlockSpec((2, share, rows, BLOCK), lambda at, pos_ref: (0, 0, at, 0))]
            + [far_spec] * (2 * chunks),
            out_specs=pl.BlockSpec((rows, 4 * share, BLOCK), lambda at, pos_ref: (at, 0, 0)),
        ),
        out_shape=jax.ShapeDtypeStruct((part, 4 * share, BLOCK), F32),
        cost_estimate=pl.CostEstimate(
            flops=0, bytes_accessed=32 * share * part * BLOCK, transcendentals=0
        ),
        name="place",
    )(pos, own, *far[0], *far[1])


def layer(features, cotangent, block_weights, block_rows, block_cols, lowrank_in, lowrank_out):
    _, width = features.shape
    share = width // BLOCK
    count = WIDTH // BLOCK
    stored = block_weights.shape[0]
    chunks = min(CHUNKS, share)
    per = share // chunks
    items = lax.axis_size("items")
    item = lax.axis_index("items").astype(jnp.int32)
    item_arg = item.reshape(1)
    bits = items.bit_length() - 1
    place = lax.axis_index("wloop")
    way_bits = lax.axis_size("wloop").bit_length() - 1
    far_bits = (way_bits - 2, way_bits - 1)

    def hop(value, bit):
        return swapped(value, "wloop", bit)

    stride_of = jnp.bitwise_xor(block_rows, block_cols)
    stride_id = (stride_of == 1) * 1 + (stride_of == count // 4) * 2 + (stride_of == count // 2) * 3
    key = stride_id * share + block_cols % share
    pos = jnp.sum(
        jnp.where(
            key[None, :] == jnp.arange(4 * share, dtype=jnp.int32)[:, None],
            jnp.arange(stored, dtype=jnp.int32)[None, :],
            0,
        ),
        axis=1,
    ).astype(jnp.int32)

    far = [[], []]
    for one in range(chunks):
        piece = lax.optimization_barrier(features[:, one * per * BLOCK : (one + 1) * per * BLOCK])
        for way in range(2):
            far[way].append(hop(piece, far_bits[way]))

    unit = min(BLOCK, share * BLOCK // items)
    units = share * BLOCK // items // unit
    shares = weight_share(block_weights, pos, item_arg, share, unit, units)
    far_weights = []
    for way in range(2):
        held = hop(shares[way], far_bits[way])
        for level in range(bits - 1, -1, -1):
            held = jnp.concatenate([held, swapped(held, "items", level)], axis=0)
        far_weights.append(held)

    dims = (((1,), (1,)), ((), ()))
    codes = jnp.stack(
        [
            lax.dot_general(features, lowrank_in, dims, preferred_element_type=F32),
            lax.dot_general(cotangent, lowrank_out, dims, preferred_element_type=F32),
        ]
    )
    for level in range(way_bits - 1):
        mine = (place >> level) & 1
        split = codes.reshape(2, 2, codes.shape[1] // 2, codes.shape[2])
        codes = pick(split, mine, 1) + hop(pick(split, 1 - mine, 1), level)
    codes = codes + hop(codes, way_bits - 1)
    codes = codes.astype(BF16)
    for level in range(way_bits - 2, -1, -1):
        mine = (place >> level) & 1
        other = hop(codes, level)
        codes = jnp.where(
            mine == 0,
            jnp.concatenate([codes, other], axis=1),
            jnp.concatenate([other, codes], axis=1),
        )
    codes, backs = codes[0], codes[1]

    bit = item_arg & 1
    own = pair_grads(bit, cotangent, [features], ((0, 0), (0, 1)), 0, share, items)
    own = items_sum(*own, item)
    returned = [[], []]
    for one in range(chunks):
        pairs = pair_grads(
            bit,
            cotangent,
            [far[0][one], far[1][one]],
            ((0, 0), (1, 0)),
            one * per,
            per,
            items,
        )
        done = items_sum(*pairs, item).astype(BF16)
        for way in range(2):
            returned[way].append(hop(done[way], far_bits[way]))

    low = items_sum(*low_kernel(bit, backs, features, codes, cotangent, items), item)

    mixed = mixed_kernel(
        features,
        block_weights,
        codes,
        lowrank_out,
        far,
        far_weights,
        pos,
        item_arg,
        units,
        bits,
    )
    block_grads = place_kernel(own, returned, pos)
    return (mixed, block_grads, low[0], low[1])


def solution(mesh):
    return jax.shard_map(
        layer,
        mesh=mesh,
        in_specs=(
            P(("groups", "items"), "wloop"),
            P(("groups", "items"), "wloop"),
            P("wloop", None, None),
            P("wloop"),
            P("wloop"),
            P(None, "wloop"),
            P(None, "wloop"),
        ),
        out_specs=(
            P(("groups", "items"), "wloop"),
            P(("groups", "items"), "wloop", None),
            P(("groups", "items"), "wloop"),
            P(("groups", "items"), "wloop"),
        ),
        check_vma=False,
    )
```

```python
import functools

import jax
import jax.numpy as jnp
from jax import lax
from jax.experimental import pallas as pl
from jax.experimental.pallas import tpu as pltpu
from jax.sharding import PartitionSpec as P


WIDTH = 16384
BLOCK = 256
CHUNK_SIZES = (4, 4, 4, 4)


F32 = jnp.float32
BF16 = jnp.bfloat16


def swapped(block, axis, apart):
    count = lax.axis_size(axis)
    return lax.ppermute(block, axis, [(one, one ^ (1 << apart)) for one in range(count)])


def after(value, *deps):
    return lax.optimization_barrier((value, *deps))[0]


def pick(values, index, dim):
    return lax.dynamic_index_in_dim(values, index, dim, keepdims=False)


def grad_body(pairs, part, bit_ref, g_ref, *refs):
    f_refs, (send_ref, keep_ref, acc_ref) = refs[:-3], refs[-3:]
    bit = bit_ref[0]
    blocks = g_ref.shape[1] // BLOCK
    halves = send_ref.shape[0]
    for at in range(blocks):
        for slot, (f_at, flip) in enumerate(pairs):
            g_at = at ^ flip
            acc_ref[...] = lax.dot_general(
                g_ref[:, g_at * BLOCK : (g_at + 1) * BLOCK],
                f_refs[f_at][:, at * BLOCK : (at + 1) * BLOCK],
                (((0,), (0,)), ((), ())),
                preferred_element_type=F32,
            )
            for half in range(halves):
                first = pl.multiple_of((2 * half + bit) * part, part)
                other = pl.multiple_of((2 * half + 1 - bit) * part, part)
                keep_ref[half, slot, at] = acc_ref[pl.ds(first, part), :]
                send_ref[half, slot, at] = acc_ref[pl.ds(other, part), :].astype(BF16)


def pair_grads(bit, cotangent, features, pairs, first, count, parts):
    rows_here = cotangent.shape[0]
    part = BLOCK // parts
    step = min(2, count)
    shape = (parts // 2, 2, count, part, BLOCK)
    block = (parts // 2, 2, step, part, BLOCK)
    out_spec = pl.BlockSpec(block, lambda at, bit_ref: (0, 0, at, 0, 0))
    skip = first // step
    return pl.pallas_call(
        functools.partial(grad_body, pairs, part),
        grid_spec=pltpu.PrefetchScalarGridSpec(
            num_scalar_prefetch=1,
            grid=(count // step,),
            in_specs=[pl.BlockSpec((rows_here, step * BLOCK), lambda at, bit_ref: (0, at + skip))]
            + [pl.BlockSpec((rows_here, step * BLOCK), lambda at, bit_ref: (0, at))] * len(features),
            out_specs=(out_spec, out_spec),
            scratch_shapes=[pltpu.VMEM((BLOCK, BLOCK), F32)],
        ),
        out_shape=(jax.ShapeDtypeStruct(shape, BF16), jax.ShapeDtypeStruct(shape, F32)),
        cost_estimate=pl.CostEstimate(
            flops=4 * count * rows_here * BLOCK * BLOCK,
            bytes_accessed=count * BLOCK * (2 * rows_here * 3 + 6 * BLOCK),
            transcendentals=0,
        ),
        name="pair_grads",
    )(bit, cotangent, *features)


def low_body(part, bit_ref, b_ref, f_ref, c_ref, g_ref, send_ref, keep_ref, acc_ref):
    bit = bit_ref[0]
    for slot, (small, wide) in enumerate(((b_ref, f_ref), (c_ref, g_ref))):
        acc_ref[...] = lax.dot_general(
            small[...], wide[...], (((0,), (0,)), ((), ())), preferred_element_type=F32
        )
        for half in range(send_ref.shape[0]):
            first = pl.multiple_of((2 * half + bit) * part, part)
            other = pl.multiple_of((2 * half + 1 - bit) * part, part)
            keep_ref[half, slot] = acc_ref[pl.ds(first, part), :]
            send_ref[half, slot] = acc_ref[pl.ds(other, part), :].astype(BF16)


def low_kernel(bit, backs, features, codes, cotangent, parts):
    rows_here, width = features.shape
    rank = codes.shape[1]
    part = rank // parts
    step = min(1024, width)
    out_spec = pl.BlockSpec((parts // 2, 2, part, step), lambda at, bit_ref: (0, 0, 0, at))
    shape = (parts // 2, 2, part, width)
    wide = pl.BlockSpec((rows_here, step), lambda at, bit_ref: (0, at))
    small = pl.BlockSpec((rows_here, rank), lambda at, bit_ref: (0, 0))
    return pl.pallas_call(
        functools.partial(low_body, part),
        grid_spec=pltpu.PrefetchScalarGridSpec(
            num_scalar_prefetch=1,
            grid=(width // step,),
            in_specs=[small, wide, small, wide],
            out_specs=(out_spec, out_spec),
            scratch_shapes=[pltpu.VMEM((rank, step), F32)],
        ),
        out_shape=(jax.ShapeDtypeStruct(shape, BF16), jax.ShapeDtypeStruct(shape, F32)),
        cost_estimate=pl.CostEstimate(
            flops=4 * rank * rows_here * width,
            bytes_accessed=width * (4 * rows_here + 6 * rank),
            transcendentals=0,
        ),
        name="low_grads",
    )(bit, backs, features, codes, cotangent)


def items_sum(send, keep, index):
    bits = lax.axis_size("items").bit_length() - 1
    came = swapped(send, "items", 0)
    for level in range(1, bits):
        mine = (index >> level) & 1
        shape = (keep.shape[0] // 2, 2, *keep.shape[1:])
        keep, came = keep.reshape(shape), came.reshape(shape)
        leave = pick(keep, 1 - mine, 1) + pick(came, 1 - mine, 1).astype(F32)
        keep = pick(keep, mine, 1) + pick(came, mine, 1).astype(F32)
        came = swapped(leave.astype(BF16), "items", level)
    return keep[0], came[0]


def share_body(share, units, unit, pos_ref, item_ref, w_ref, out_ref, sems):
    pieces = BLOCK // unit
    copies = []
    for way in range(2):
        for one in range(units):
            number = item_ref[0] * units + one
            block = pos_ref[(2 + way) * share + lax.div(number, pieces)]
            first = pl.multiple_of(lax.rem(number, pieces) * unit, unit)
            copies.append(
                pltpu.make_async_copy(
                    w_ref.at[block, pl.ds(first, unit), :],
                    out_ref.at[way, one],
                    sems.at[way * units + one],
                )
            )
    for copy in copies:
        copy.start()
    for copy in copies:
        copy.wait()


def weight_share(block_weights, pos, item, share, unit, units):
    return pl.pallas_call(
        functools.partial(share_body, share, units, unit),
        in_specs=[
            pl.BlockSpec(memory_space=pltpu.SMEM),
            pl.BlockSpec(memory_space=pltpu.SMEM),
            pl.BlockSpec(memory_space=pl.ANY),
        ],
        out_specs=pl.BlockSpec(memory_space=pltpu.VMEM),
        out_shape=jax.ShapeDtypeStruct((2, units, unit, BLOCK), BF16),
        scratch_shapes=[pltpu.SemaphoreType.DMA((2 * units,))],
        cost_estimate=pl.CostEstimate(
            flops=0, bytes_accessed=8 * units * unit * BLOCK, transcendentals=0
        ),
        name="weight_share",
    )(pos, item, block_weights)


def mixed_body(share, sizes, first, last, units, unit, order, pos_ref, item_ref, f_ref, w_ref, codes_ref, low_ref, *refs):
    steps = last - first
    far_refs, refs = refs[: 2 * steps], refs[2 * steps :]
    parts = len(order)
    far_w, refs = refs[: 2 * parts], refs[2 * parts :]
    out_ref, f_buf, low_buf, far_buf, w_buf, out_buf, in_sems, w_sems, far_w_sems, out_sems = refs[-10:]
    dims = (((1,), (1,)), ((), ()))
    pieces = BLOCK // unit
    item = item_ref[0]
    starts = [sum(sizes[:one]) for one in range(len(sizes))]

    gathered = []
    for way in range(2):
        for slot, apart in enumerate(order):
            owner = item ^ apart
            source = far_w[way * parts + slot]
            if pieces == 1:
                into = w_buf.at[2 + way, pl.ds(owner * units, units)]
            else:
                rows = pl.ds(pl.multiple_of(lax.rem(owner, pieces) * unit, unit), unit)
                source = source.at[0]
                into = w_buf.at[2 + way, lax.div(owner, pieces), rows, :]
            gathered.append(pltpu.make_async_copy(source, into, far_w_sems.at[way, slot]))
    loads = []
    for step in range(steps):
        chunk = first + step
        cols = pl.ds(starts[chunk] * BLOCK, sizes[chunk] * BLOCK)
        copies = [
            pltpu.make_async_copy(f_ref.at[:, cols], f_buf.at[:, cols], in_sems.at[step, 0]),
            pltpu.make_async_copy(low_ref.at[:, cols], low_buf.at[:, cols], in_sems.at[step, 1]),
        ]
        for way in range(2):
            copies.append(
                pltpu.make_async_copy(
                    far_refs[way * steps + step], far_buf.at[way, :, cols], in_sems.at[step, 2 + way]
                )
            )
        for at in range(starts[chunk], starts[chunk] + sizes[chunk]):
            copies.append(
                pltpu.make_async_copy(w_ref.at[pos_ref[at]], w_buf.at[0, at], w_sems.at[0, at])
            )
            copies.append(
                pltpu.make_async_copy(
                    w_ref.at[pos_ref[share + (at ^ 1)]], w_buf.at[1, at], w_sems.at[1, at]
                )
            )
        loads.append(copies)
    for copy in gathered:
        copy.start()
    for copies in loads:
        for copy in copies:
            copy.start()
    for copy in gathered:
        copy.wait()
    stores = []
    for step in range(steps):
        chunk = first + step
        for copy in loads[step]:
            copy.wait()
        for at in range(starts[chunk], starts[chunk] + sizes[chunk]):
            own = slice(at * BLOCK, (at + 1) * BLOCK)
            flip = slice((at ^ 1) * BLOCK, ((at ^ 1) + 1) * BLOCK)
            total = lax.dot_general(f_buf[:, own], w_buf[0, at], dims, preferred_element_type=F32)
            total += lax.dot_general(f_buf[:, flip], w_buf[1, at], dims, preferred_element_type=F32)
            for way in range(2):
                total += lax.dot_general(
                    far_buf[way, :, own], w_buf[2 + way, at], dims, preferred_element_type=F32
                )
            total += jnp.dot(codes_ref[...], low_buf[:, own], preferred_element_type=F32)
            out_buf[:, own] = total.astype(BF16)
        cols = pl.ds(starts[chunk] * BLOCK, sizes[chunk] * BLOCK)
        store = pltpu.make_async_copy(out_buf.at[:, cols], out_ref.at[:, cols], out_sems.at[step])
        store.start()
        stores.append(store)
    for store in stores:
        store.wait()


def mixed_kernel(
    features, block_weights, codes, lowrank_out, far, far_weights, pos, item, sizes, first, last, units, order, held
):
    rows_here, width = features.shape
    share = width // BLOCK
    unit = far_weights[0][0].shape[1]
    hbm = pl.BlockSpec(memory_space=pl.ANY)
    smem = pl.BlockSpec(memory_space=pltpu.SMEM)
    far_inputs = [*far[0][first:last], *far[1][first:last], *far_weights[0], *far_weights[1]]
    inputs = [pos, item, features, block_weights, codes, lowrank_out, *far_inputs]
    if held is not None:
        inputs.append(held)
    columns = sum(sizes[first:last])
    return pl.pallas_call(
        functools.partial(mixed_body, share, sizes, first, last, units, unit, order),
        in_specs=[smem, smem, hbm, hbm, pl.BlockSpec(memory_space=pltpu.VMEM), hbm]
        + [hbm] * (len(inputs) - 6),
        out_specs=hbm,
        out_shape=jax.ShapeDtypeStruct((rows_here, width), BF16),
        input_output_aliases={} if held is None else {len(inputs) - 1: 0},
        scratch_shapes=[
            pltpu.VMEM((rows_here, width), BF16),
            pltpu.VMEM(lowrank_out.shape, BF16),
            pltpu.VMEM((2, rows_here, width), BF16),
            pltpu.VMEM((4, share, BLOCK, BLOCK), BF16),
            pltpu.VMEM((rows_here, width), BF16),
            pltpu.SemaphoreType.DMA((last - first, 4)),
            pltpu.SemaphoreType.DMA((2, share)),
            pltpu.SemaphoreType.DMA((2, len(order))),
            pltpu.SemaphoreType.DMA((last - first,)),
        ],
        cost_estimate=pl.CostEstimate(
            flops=9 * columns * rows_here * BLOCK * BLOCK,
            bytes_accessed=columns * BLOCK * 2 * (4 * rows_here + 4 * BLOCK),
            transcendentals=0,
        ),
        name="mixed",
    )(*inputs)


def place_body(share, sizes, pos_ref, own_ref, *refs):
    far_refs, out_ref = refs[:-1], refs[-1]
    chunks = len(sizes)
    for way in range(4):
        for chunk in range(chunks):
            first = sum(sizes[:chunk])
            for at in range(first, first + sizes[chunk]):
                if way < 2:
                    block = own_ref[way, at]
                else:
                    block = far_refs[(way - 2) * chunks + chunk][at - first].astype(F32)
                out_ref[:, pos_ref[way * share + at], :] = block


def place_kernel(own, far, pos, sizes):
    _, share, part, _ = own.shape
    rows = 16
    far_specs = [
        pl.BlockSpec((size, rows, BLOCK), lambda at, pos_ref: (0, at, 0)) for size in sizes
    ]
    return pl.pallas_call(
        functools.partial(place_body, share, sizes),
        grid_spec=pltpu.PrefetchScalarGridSpec(
            num_scalar_prefetch=1,
            grid=(part // rows,),
            in_specs=[pl.BlockSpec((2, share, rows, BLOCK), lambda at, pos_ref: (0, 0, at, 0))]
            + far_specs
            + far_specs,
            out_specs=pl.BlockSpec((rows, 4 * share, BLOCK), lambda at, pos_ref: (at, 0, 0)),
        ),
        out_shape=jax.ShapeDtypeStruct((part, 4 * share, BLOCK), F32),
        cost_estimate=pl.CostEstimate(
            flops=0, bytes_accessed=32 * share * part * BLOCK, transcendentals=0
        ),
        name="place",
    )(pos, own, *far[0], *far[1])


def layer(features, cotangent, block_weights, block_rows, block_cols, lowrank_in, lowrank_out):
    _, width = features.shape
    share = width // BLOCK
    count = WIDTH // BLOCK
    stored = block_weights.shape[0]
    sizes = chunk_sizes(share)
    chunks = len(sizes)
    items = lax.axis_size("items")
    item = lax.axis_index("items").astype(jnp.int32)
    item_arg = item.reshape(1)
    bits = items.bit_length() - 1
    place = lax.axis_index("wloop")
    way_bits = lax.axis_size("wloop").bit_length() - 1
    far_bits = (way_bits - 2, way_bits - 1)

    def hop(value, bit):
        return swapped(value, "wloop", bit)

    stride_of = jnp.bitwise_xor(block_rows, block_cols)
    stride_id = (stride_of == 1) * 1 + (stride_of == count // 4) * 2 + (stride_of == count // 2) * 3
    key = stride_id * share + block_cols % share
    pos = jnp.sum(
        jnp.where(
            key[None, :] == jnp.arange(4 * share, dtype=jnp.int32)[:, None],
            jnp.arange(stored, dtype=jnp.int32)[None, :],
            0,
        ),
        axis=1,
    ).astype(jnp.int32)

    far, source = [[], []], features
    for one in range(chunks):
        first = sum(sizes[:one]) * BLOCK
        piece = source[:, first : first + sizes[one] * BLOCK]
        if one + 1 < chunks:
            source = after(source, far[1][-1] if far[1] else piece)
        for way in range(2):
            far[way].append(hop(piece, far_bits[way]))

    unit = min(BLOCK, share * BLOCK // items)
    units = share * BLOCK // items // unit
    shares = weight_share(block_weights, pos, item_arg, share, unit, units)
    far_weights, order = [], []
    for way in range(2):
        held, order = [hop(shares[way], far_bits[way])], [0]
        for level in range(bits - 1, -1, -1):
            for one in range(len(held)):
                held.append(swapped(held[one], "items", level))
                order.append(order[one] ^ (1 << level))
        far_weights.append(held)

    dims = (((1,), (1,)), ((), ()))
    codes = jnp.stack(
        [
            lax.dot_general(features, lowrank_in, dims, preferred_element_type=F32),
            lax.dot_general(cotangent, lowrank_out, dims, preferred_element_type=F32),
        ]
    )
    for level in range(way_bits - 1):
        mine = (place >> level) & 1
        split = codes.reshape(2, 2, codes.shape[1] // 2, codes.shape[2])
        codes = pick(split, mine, 1) + hop(pick(split, 1 - mine, 1), level)
    came = hop(codes, way_bits - 1)
    codes = (codes + came).astype(BF16)
    for level in range(way_bits - 2, -1, -1):
        mine = (place >> level) & 1
        other = hop(codes, level)
        codes = jnp.where(
            mine == 0,
            jnp.concatenate([codes, other], axis=1),
            jnp.concatenate([other, codes], axis=1),
        )
    codes, backs = codes[0], codes[1]

    bit = item_arg & 1
    own = pair_grads(bit, cotangent, [features], ((0, 0), (0, 1)), 0, share, items)
    own = items_sum(*own, item)
    own = own[0] + own[1].astype(F32)
    returned = [[], []]
    for one in range(chunks):
        pairs = pair_grads(
            bit,
            cotangent,
            [far[0][one], far[1][one]],
            ((0, 0), (1, 0)),
            sum(sizes[:one]),
            sizes[one],
            items,
        )
        keep, came = items_sum(*pairs, item)
        for way in range(2):
            done = (keep[way] + came[way].astype(F32)).astype(BF16)
            returned[way].append(hop(done, far_bits[way]))

    low = low_kernel(bit, backs, features, codes, cotangent, items)
    keep, came = items_sum(*low, item)
    low = [keep[way] + came[way].astype(F32) for way in range(2)]

    mixed = None
    for first, last in ((0, chunks - 1), (chunks - 1, chunks)):
        mixed = mixed_kernel(
            features,
            block_weights,
            codes,
            lowrank_out,
            far,
            far_weights,
            pos,
            item_arg,
            sizes,
            first,
            last,
            units,
            order,
            mixed,
        )
    block_grads = place_kernel(own, returned, pos, sizes)
    return (mixed, block_grads, low[0], low[1])


def chunk_sizes(share):
    return CHUNK_SIZES if sum(CHUNK_SIZES) == share else (1,) * share


def solution(mesh):
    return jax.shard_map(
        layer,
        mesh=mesh,
        in_specs=(
            P(("groups", "items"), "wloop"),
            P(("groups", "items"), "wloop"),
            P("wloop", None, None),
            P("wloop"),
            P("wloop"),
            P(None, "wloop"),
            P(None, "wloop"),
        ),
        out_specs=(
            P(("groups", "items"), "wloop"),
            P(("groups", "items"), "wloop", None),
            P(("groups", "items"), "wloop"),
            P(("groups", "items"), "wloop"),
        ),
        check_vma=False,
    )
```

```python
import functools

import jax
import jax.numpy as jnp
from jax import lax
from jax.experimental import pallas as pl
from jax.experimental.pallas import tpu as pltpu
from jax.sharding import PartitionSpec as P


WIDTH = 16384
BLOCK = 256
CHUNK_SIZES = (4, 6, 4, 2)
EARLY_CHUNKS = 2


F32 = jnp.float32
BF16 = jnp.bfloat16


def swapped(block, axis, apart):
    count = lax.axis_size(axis)
    return lax.ppermute(block, axis, [(one, one ^ (1 << apart)) for one in range(count)])


def after(value, *deps):
    return lax.optimization_barrier((value, *deps))[0]


def pick(values, index, dim):
    return lax.dynamic_index_in_dim(values, index, dim, keepdims=False)


def grad_body(pairs, part, bit_ref, g_ref, *refs):
    f_refs, (send_ref, keep_ref, acc_ref) = refs[:-3], refs[-3:]
    bit = bit_ref[0]
    blocks = g_ref.shape[1] // BLOCK
    halves = send_ref.shape[0]
    for at in range(blocks):
        for slot, (f_at, flip) in enumerate(pairs):
            g_at = at ^ flip
            acc_ref[...] = lax.dot_general(
                g_ref[:, g_at * BLOCK : (g_at + 1) * BLOCK],
                f_refs[f_at][:, at * BLOCK : (at + 1) * BLOCK],
                (((0,), (0,)), ((), ())),
                preferred_element_type=F32,
            )
            for half in range(halves):
                first = pl.multiple_of((2 * half + bit) * part, part)
                other = pl.multiple_of((2 * half + 1 - bit) * part, part)
                keep_ref[half, slot, at] = acc_ref[pl.ds(first, part), :]
                send_ref[half, slot, at] = acc_ref[pl.ds(other, part), :].astype(BF16)


def pair_grads(bit, cotangent, features, pairs, first, count, parts):
    rows_here = cotangent.shape[0]
    part = BLOCK // parts
    step = min(2, count)
    shape = (parts // 2, 2, count, part, BLOCK)
    block = (parts // 2, 2, step, part, BLOCK)
    out_spec = pl.BlockSpec(block, lambda at, bit_ref: (0, 0, at, 0, 0))
    skip = first // step
    return pl.pallas_call(
        functools.partial(grad_body, pairs, part),
        grid_spec=pltpu.PrefetchScalarGridSpec(
            num_scalar_prefetch=1,
            grid=(count // step,),
            in_specs=[pl.BlockSpec((rows_here, step * BLOCK), lambda at, bit_ref: (0, at + skip))]
            + [pl.BlockSpec((rows_here, step * BLOCK), lambda at, bit_ref: (0, at))] * len(features),
            out_specs=(out_spec, out_spec),
            scratch_shapes=[pltpu.VMEM((BLOCK, BLOCK), F32)],
        ),
        out_shape=(jax.ShapeDtypeStruct(shape, BF16), jax.ShapeDtypeStruct(shape, F32)),
        cost_estimate=pl.CostEstimate(
            flops=4 * count * rows_here * BLOCK * BLOCK,
            bytes_accessed=count * BLOCK * (2 * rows_here * 3 + 6 * BLOCK),
            transcendentals=0,
        ),
        name="pair_grads",
    )(bit, cotangent, *features)


def low_body(part, bit_ref, b_ref, f_ref, c_ref, g_ref, send_ref, keep_ref, acc_ref):
    bit = bit_ref[0]
    for slot, (small, wide) in enumerate(((b_ref, f_ref), (c_ref, g_ref))):
        acc_ref[...] = lax.dot_general(
            small[...], wide[...], (((0,), (0,)), ((), ())), preferred_element_type=F32
        )
        for half in range(send_ref.shape[0]):
            first = pl.multiple_of((2 * half + bit) * part, part)
            other = pl.multiple_of((2 * half + 1 - bit) * part, part)
            keep_ref[half, slot] = acc_ref[pl.ds(first, part), :]
            send_ref[half, slot] = acc_ref[pl.ds(other, part), :].astype(BF16)


def low_kernel(bit, backs, features, codes, cotangent, parts):
    rows_here, width = features.shape
    rank = codes.shape[1]
    part = rank // parts
    step = min(1024, width)
    out_spec = pl.BlockSpec((parts // 2, 2, part, step), lambda at, bit_ref: (0, 0, 0, at))
    shape = (parts // 2, 2, part, width)
    wide = pl.BlockSpec((rows_here, step), lambda at, bit_ref: (0, at))
    small = pl.BlockSpec((rows_here, rank), lambda at, bit_ref: (0, 0))
    return pl.pallas_call(
        functools.partial(low_body, part),
        grid_spec=pltpu.PrefetchScalarGridSpec(
            num_scalar_prefetch=1,
            grid=(width // step,),
            in_specs=[small, wide, small, wide],
            out_specs=(out_spec, out_spec),
            scratch_shapes=[pltpu.VMEM((rank, step), F32)],
        ),
        out_shape=(jax.ShapeDtypeStruct(shape, BF16), jax.ShapeDtypeStruct(shape, F32)),
        cost_estimate=pl.CostEstimate(
            flops=4 * rank * rows_here * width,
            bytes_accessed=width * (4 * rows_here + 6 * rank),
            transcendentals=0,
        ),
        name="low_grads",
    )(bit, backs, features, codes, cotangent)


def items_sum(send, keep, index):
    bits = lax.axis_size("items").bit_length() - 1
    came = swapped(send, "items", 0)
    for level in range(1, bits):
        mine = (index >> level) & 1
        shape = (keep.shape[0] // 2, 2, *keep.shape[1:])
        keep, came = keep.reshape(shape), came.reshape(shape)
        leave = pick(keep, 1 - mine, 1) + pick(came, 1 - mine, 1).astype(F32)
        keep = pick(keep, mine, 1) + pick(came, mine, 1).astype(F32)
        came = swapped(leave.astype(BF16), "items", level)
    return keep[0], came[0]


def share_body(share, units, unit, pos_ref, item_ref, w_ref, *refs):
    out_refs, sems = refs[:2], refs[2]
    pieces = BLOCK // unit
    copies = []
    for way in range(2):
        for one in range(units):
            number = item_ref[0] * units + one
            block = pos_ref[(2 + way) * share + lax.div(number, pieces)]
            first = pl.multiple_of(lax.rem(number, pieces) * unit, unit)
            copies.append(
                pltpu.make_async_copy(
                    w_ref.at[block, pl.ds(first, unit), :],
                    out_refs[way].at[one],
                    sems.at[way * units + one],
                )
            )
    for copy in copies:
        copy.start()
    for copy in copies:
        copy.wait()


def weight_share(block_weights, pos, item, share, unit, units):
    return pl.pallas_call(
        functools.partial(share_body, share, units, unit),
        in_specs=[
            pl.BlockSpec(memory_space=pltpu.SMEM),
            pl.BlockSpec(memory_space=pltpu.SMEM),
            pl.BlockSpec(memory_space=pl.ANY),
        ],
        out_specs=(pl.BlockSpec(memory_space=pltpu.VMEM),) * 2,
        out_shape=(jax.ShapeDtypeStruct((units, unit, BLOCK), BF16),) * 2,
        scratch_shapes=[pltpu.SemaphoreType.DMA((2 * units,))],
        cost_estimate=pl.CostEstimate(
            flops=0, bytes_accessed=8 * units * unit * BLOCK, transcendentals=0
        ),
        name="weight_share",
    )(pos, item, block_weights)


def mixed_body(share, sizes, first, last, units, unit, order, pos_ref, item_ref, f_ref, w_ref, codes_ref, low_ref, *refs):
    steps = last - first
    far_refs, refs = refs[: 2 * steps], refs[2 * steps :]
    parts = len(order)
    far_w, refs = refs[: 2 * parts], refs[2 * parts :]
    out_ref, f_buf, low_buf, far_buf, w_buf, out_buf, in_sems, w_sems, far_w_sems, out_sems = refs[-10:]
    dims = (((1,), (1,)), ((), ()))
    pieces = BLOCK // unit
    item = item_ref[0]
    starts = [sum(sizes[:one]) for one in range(len(sizes))]

    gathered = []
    for way in range(2):
        for slot, apart in enumerate(order):
            owner = item ^ apart
            source = far_w[way * parts + slot]
            if pieces == 1:
                into = w_buf.at[2 + way, pl.ds(owner * units, units)]
            else:
                rows = pl.ds(pl.multiple_of(lax.rem(owner, pieces) * unit, unit), unit)
                source = source.at[0]
                into = w_buf.at[2 + way, lax.div(owner, pieces), rows, :]
            gathered.append(pltpu.make_async_copy(source, into, far_w_sems.at[way, slot]))
    loads = []
    for step in range(steps):
        chunk = first + step
        cols = pl.ds(starts[chunk] * BLOCK, sizes[chunk] * BLOCK)
        copies = [
            pltpu.make_async_copy(f_ref.at[:, cols], f_buf.at[:, cols], in_sems.at[step, 0]),
            pltpu.make_async_copy(low_ref.at[:, cols], low_buf.at[:, cols], in_sems.at[step, 1]),
        ]
        for way in range(2):
            copies.append(
                pltpu.make_async_copy(
                    far_refs[way * steps + step], far_buf.at[way, :, cols], in_sems.at[step, 2 + way]
                )
            )
        for at in range(starts[chunk], starts[chunk] + sizes[chunk]):
            copies.append(
                pltpu.make_async_copy(w_ref.at[pos_ref[at]], w_buf.at[0, at], w_sems.at[0, at])
            )
            copies.append(
                pltpu.make_async_copy(
                    w_ref.at[pos_ref[share + (at ^ 1)]], w_buf.at[1, at], w_sems.at[1, at]
                )
            )
        loads.append(copies)
    for copy in gathered:
        copy.start()
    for copies in loads:
        for copy in copies:
            copy.start()
    for copy in gathered:
        copy.wait()
    stores = []
    for step in range(steps):
        chunk = first + step
        for copy in loads[step]:
            copy.wait()
        for at in range(starts[chunk], starts[chunk] + sizes[chunk]):
            own = slice(at * BLOCK, (at + 1) * BLOCK)
            flip = slice((at ^ 1) * BLOCK, ((at ^ 1) + 1) * BLOCK)
            total = lax.dot_general(f_buf[:, own], w_buf[0, at], dims, preferred_element_type=F32)
            total += lax.dot_general(f_buf[:, flip], w_buf[1, at], dims, preferred_element_type=F32)
            for way in range(2):
                total += lax.dot_general(
                    far_buf[way, :, own], w_buf[2 + way, at], dims, preferred_element_type=F32
                )
            total += jnp.dot(codes_ref[...], low_buf[:, own], preferred_element_type=F32)
            out_buf[:, own] = total.astype(BF16)
        cols = pl.ds(starts[chunk] * BLOCK, sizes[chunk] * BLOCK)
        store = pltpu.make_async_copy(out_buf.at[:, cols], out_ref.at[:, cols], out_sems.at[step])
        store.start()
        stores.append(store)
    for store in stores:
        store.wait()


def mixed_kernel(
    features, block_weights, codes, lowrank_out, far, far_weights, pos, item, sizes, first, last, units, order, held
):
    rows_here, width = features.shape
    share = width // BLOCK
    unit = far_weights[0][0].shape[1]
    hbm = pl.BlockSpec(memory_space=pl.ANY)
    smem = pl.BlockSpec(memory_space=pltpu.SMEM)
    far_inputs = [*far[0][first:last], *far[1][first:last], *far_weights[0], *far_weights[1]]
    inputs = [pos, item, features, block_weights, codes, lowrank_out, *far_inputs]
    if held is not None:
        inputs.append(held)
    columns = sum(sizes[first:last])
    return pl.pallas_call(
        functools.partial(mixed_body, share, sizes, first, last, units, unit, order),
        in_specs=[smem, smem, hbm, hbm, pl.BlockSpec(memory_space=pltpu.VMEM), hbm]
        + [hbm] * (len(inputs) - 6),
        out_specs=hbm,
        out_shape=jax.ShapeDtypeStruct((rows_here, width), BF16),
        input_output_aliases={} if held is None else {len(inputs) - 1: 0},
        scratch_shapes=[
            pltpu.VMEM((rows_here, width), BF16),
            pltpu.VMEM(lowrank_out.shape, BF16),
            pltpu.VMEM((2, rows_here, width), BF16),
            pltpu.VMEM((4, share, BLOCK, BLOCK), BF16),
            pltpu.VMEM((rows_here, width), BF16),
            pltpu.SemaphoreType.DMA((last - first, 4)),
            pltpu.SemaphoreType.DMA((2, share)),
            pltpu.SemaphoreType.DMA((2, len(order))),
            pltpu.SemaphoreType.DMA((last - first,)),
        ],
        cost_estimate=pl.CostEstimate(
            flops=9 * columns * rows_here * BLOCK * BLOCK,
            bytes_accessed=columns * BLOCK * 2 * (4 * rows_here + 4 * BLOCK),
            transcendentals=0,
        ),
        name="mixed",
    )(*inputs)


def place_body(share, sizes, pos_ref, own_ref, *refs):
    far_refs, out_ref = refs[:-1], refs[-1]
    chunks = len(sizes)
    for way in range(4):
        for chunk in range(chunks):
            first = sum(sizes[:chunk])
            for at in range(first, first + sizes[chunk]):
                if way < 2:
                    block = own_ref[way, at]
                else:
                    block = far_refs[(way - 2) * chunks + chunk][at - first].astype(F32)
                out_ref[:, pos_ref[way * share + at], :] = block


def place_kernel(own, far, pos, sizes):
    _, share, part, _ = own.shape
    rows = 16
    far_specs = [
        pl.BlockSpec((size, rows, BLOCK), lambda at, pos_ref: (0, at, 0)) for size in sizes
    ]
    return pl.pallas_call(
        functools.partial(place_body, share, sizes),
        grid_spec=pltpu.PrefetchScalarGridSpec(
            num_scalar_prefetch=1,
            grid=(part // rows,),
            in_specs=[pl.BlockSpec((2, share, rows, BLOCK), lambda at, pos_ref: (0, 0, at, 0))]
            + far_specs
            + far_specs,
            out_specs=pl.BlockSpec((rows, 4 * share, BLOCK), lambda at, pos_ref: (at, 0, 0)),
        ),
        out_shape=jax.ShapeDtypeStruct((part, 4 * share, BLOCK), F32),
        cost_estimate=pl.CostEstimate(
            flops=0, bytes_accessed=32 * share * part * BLOCK, transcendentals=0
        ),
        name="place",
    )(pos, own, *far[0], *far[1])


def layer(features, cotangent, block_weights, block_rows, block_cols, lowrank_in, lowrank_out):
    _, width = features.shape
    share = width // BLOCK
    count = WIDTH // BLOCK
    stored = block_weights.shape[0]
    sizes = chunk_sizes(share)
    chunks = len(sizes)
    items = lax.axis_size("items")
    item = lax.axis_index("items").astype(jnp.int32)
    item_arg = item.reshape(1)
    bits = items.bit_length() - 1
    place = lax.axis_index("wloop")
    way_bits = lax.axis_size("wloop").bit_length() - 1
    far_bits = (way_bits - 2, way_bits - 1)

    def hop(value, bit):
        return swapped(value, "wloop", bit)

    stride_of = jnp.bitwise_xor(block_rows, block_cols)
    stride_id = (stride_of == 1) * 1 + (stride_of == count // 4) * 2 + (stride_of == count // 2) * 3
    key = stride_id * share + block_cols % share
    pos = jnp.sum(
        jnp.where(
            key[None, :] == jnp.arange(4 * share, dtype=jnp.int32)[:, None],
            jnp.arange(stored, dtype=jnp.int32)[None, :],
            0,
        ),
        axis=1,
    ).astype(jnp.int32)

    far, source = [[], []], features
    for one in range(chunks):
        first = sum(sizes[:one]) * BLOCK
        piece = source[:, first : first + sizes[one] * BLOCK]
        if one + 1 < chunks:
            source = after(source, piece)
        for way in range(2):
            far[way].append(hop(piece, far_bits[way]))

    unit = min(BLOCK, share * BLOCK // items)
    units = share * BLOCK // items // unit
    shares = weight_share(block_weights, pos, item_arg, share, unit, units)
    far_weights, order = [], []
    for way in range(2):
        held, order = [hop(shares[way], far_bits[way])], [0]
        for level in range(bits - 1, -1, -1):
            for one in range(len(held)):
                held.append(swapped(held[one], "items", level))
                order.append(order[one] ^ (1 << level))
        far_weights.append(held)

    dims = (((1,), (1,)), ((), ()))
    codes = jnp.stack(
        [
            lax.dot_general(features, lowrank_in, dims, preferred_element_type=F32),
            lax.dot_general(cotangent, lowrank_out, dims, preferred_element_type=F32),
        ]
    )
    for level in range(way_bits - 1):
        mine = (place >> level) & 1
        split = codes.reshape(2, 2, codes.shape[1] // 2, codes.shape[2])
        codes = pick(split, mine, 1) + hop(pick(split, 1 - mine, 1), level)
    came = hop(codes, way_bits - 1)
    codes = (codes + came).astype(BF16)
    for level in range(way_bits - 2, -1, -1):
        mine = (place >> level) & 1
        other = hop(codes, level)
        codes = jnp.where(
            mine == 0,
            jnp.concatenate([codes, other], axis=1),
            jnp.concatenate([other, codes], axis=1),
        )
    codes, backs = codes[0], codes[1]

    bit = item_arg & 1
    own = pair_grads(bit, cotangent, [features], ((0, 0), (0, 1)), 0, share, items)
    own = items_sum(*own, item)
    own = own[0] + own[1].astype(F32)
    returned = [[], []]
    for one in range(chunks):
        pairs = pair_grads(
            bit,
            cotangent,
            [far[0][one], far[1][one]],
            ((0, 0), (1, 0)),
            sum(sizes[:one]),
            sizes[one],
            items,
        )
        keep, came = items_sum(*pairs, item)
        for way in range(2):
            done = (keep[way] + came[way].astype(F32)).astype(BF16)
            returned[way].append(hop(done, far_bits[way]))

    low = low_kernel(bit, backs, features, codes, cotangent, items)
    keep, came = items_sum(*low, item)
    low = [keep[way] + came[way].astype(F32) for way in range(2)]

    mixed = None
    early = min(EARLY_CHUNKS, chunks - 1)
    for first, last in ((0, early), (early, chunks)):
        mixed = mixed_kernel(
            features,
            block_weights,
            codes,
            lowrank_out,
            far,
            far_weights,
            pos,
            item_arg,
            sizes,
            first,
            last,
            units,
            order,
            mixed,
        )
    block_grads = place_kernel(own, returned, pos, sizes)
    return (mixed, block_grads, low[0], low[1])


def chunk_sizes(share):
    return CHUNK_SIZES if sum(CHUNK_SIZES) == share else (1,) * share


def solution(mesh):
    return jax.shard_map(
        layer,
        mesh=mesh,
        in_specs=(
            P(("groups", "items"), "wloop"),
            P(("groups", "items"), "wloop"),
            P("wloop", None, None),
            P("wloop"),
            P("wloop"),
            P(None, "wloop"),
            P(None, "wloop"),
        ),
        out_specs=(
            P(("groups", "items"), "wloop"),
            P(("groups", "items"), "wloop", None),
            P(("groups", "items"), "wloop"),
            P(("groups", "items"), "wloop"),
        ),
        check_vma=False,
    )
```

```python
import functools

import jax
import jax.numpy as jnp
from jax import lax
from jax.experimental import pallas as pl
from jax.experimental.pallas import tpu as pltpu
from jax.sharding import PartitionSpec as P


WIDTH = 16384
BLOCK = 256
CHUNK_SIZES = (4, 4, 6, 2)
EARLY_CHUNKS = 2


F32 = jnp.float32
BF16 = jnp.bfloat16


def swapped(block, axis, apart):
    count = lax.axis_size(axis)
    return lax.ppermute(block, axis, [(one, one ^ (1 << apart)) for one in range(count)])


def after(value, *deps):
    return lax.optimization_barrier((value, *deps))[0]


def pick(values, index, dim):
    return lax.dynamic_index_in_dim(values, index, dim, keepdims=False)


def grad_body(pairs, part, first, step, bit_ref, g_ref, *refs):
    count = (len(refs) - 7) // 2
    f_refs, (send_ref, keep_ref, g_buf), refs = refs[:count], refs[count : count + 3], refs[count + 3 :]
    f_bufs, (send_buf, keep_buf, in_sems, out_sems) = refs[:count], refs[count:]
    bit = bit_ref[0]
    groups = g_buf.shape[1] // (step * BLOCK)
    halves = send_ref.shape[0]
    loads = []
    for group in range(groups):
        cols = pl.ds(group * step * BLOCK, step * BLOCK)
        there = pl.ds((first + group * step) * BLOCK, step * BLOCK)
        loads.append(
            [pltpu.make_async_copy(g_ref.at[:, there], g_buf.at[:, cols], in_sems.at[group, 0])]
            + [
                pltpu.make_async_copy(
                    f_refs[one].at[:, cols], f_bufs[one].at[:, cols], in_sems.at[group, 1 + one]
                )
                for one in range(count)
            ]
        )
    for copies in loads:
        for copy in copies:
            copy.start()
    stores = []
    for group in range(groups):
        for copy in loads[group]:
            copy.wait()
        for at in range(group * step, (group + 1) * step):
            for slot, (f_at, flip) in enumerate(pairs):
                g_at = at ^ flip
                total = lax.dot_general(
                    g_buf[:, g_at * BLOCK : (g_at + 1) * BLOCK],
                    f_bufs[f_at][:, at * BLOCK : (at + 1) * BLOCK],
                    (((0,), (0,)), ((), ())),
                    preferred_element_type=F32,
                )
                for half in range(halves):
                    low = total[2 * half * part : (2 * half + 1) * part]
                    high = total[(2 * half + 1) * part : (2 * half + 2) * part]
                    keep_buf[half, slot, at] = jnp.where(bit == 0, low, high)
                    send_buf[half, slot, at] = jnp.where(bit == 0, high, low).astype(BF16)
        span = pl.ds(group * step, step)
        for which, (buf, ref) in enumerate(((send_buf, send_ref), (keep_buf, keep_ref))):
            copy = pltpu.make_async_copy(
                buf.at[:, :, span], ref.at[:, :, span], out_sems.at[group, which]
            )
            copy.start()
            stores.append(copy)
    for copy in stores:
        copy.wait()


def pair_grads(bit, cotangent, features, pairs, first, count, parts):
    rows_here = cotangent.shape[0]
    part = BLOCK // parts
    step = 2 if count % 2 == 0 else 1
    shape = (parts // 2, 2, count, part, BLOCK)
    wide = pltpu.VMEM((rows_here, count * BLOCK), BF16)
    hbm = pl.BlockSpec(memory_space=pltpu.HBM)
    return pl.pallas_call(
        functools.partial(grad_body, pairs, part, first, step),
        in_specs=[pl.BlockSpec(memory_space=pltpu.SMEM)] + [hbm] * (1 + len(features)),
        out_specs=(hbm, hbm),
        scratch_shapes=[wide] * (1 + len(features))
        + [
            pltpu.VMEM(shape, BF16),
            pltpu.VMEM(shape, F32),
            pltpu.SemaphoreType.DMA((count // step, 1 + len(features))),
            pltpu.SemaphoreType.DMA((count // step, 2)),
        ],
        out_shape=(jax.ShapeDtypeStruct(shape, BF16), jax.ShapeDtypeStruct(shape, F32)),
        cost_estimate=pl.CostEstimate(
            flops=4 * count * rows_here * BLOCK * BLOCK,
            bytes_accessed=count * BLOCK * (2 * rows_here * 3 + 6 * BLOCK),
            transcendentals=0,
        ),
        name="pair_grads",
    )(bit, cotangent, *features)


def low_body(part, bit_ref, b_ref, f_ref, c_ref, g_ref, send_ref, keep_ref, acc_ref):
    bit = bit_ref[0]
    for slot, (small, wide) in enumerate(((b_ref, f_ref), (c_ref, g_ref))):
        acc_ref[...] = lax.dot_general(
            small[...], wide[...], (((0,), (0,)), ((), ())), preferred_element_type=F32
        )
        for half in range(send_ref.shape[0]):
            first = pl.multiple_of((2 * half + bit) * part, part)
            other = pl.multiple_of((2 * half + 1 - bit) * part, part)
            keep_ref[half, slot] = acc_ref[pl.ds(first, part), :]
            send_ref[half, slot] = acc_ref[pl.ds(other, part), :].astype(BF16)


def low_kernel(bit, backs, features, codes, cotangent, parts):
    rows_here, width = features.shape
    rank = codes.shape[1]
    part = rank // parts
    step = min(1024, width)
    out_spec = pl.BlockSpec((parts // 2, 2, part, step), lambda at, bit_ref: (0, 0, 0, at))
    shape = (parts // 2, 2, part, width)
    wide = pl.BlockSpec((rows_here, step), lambda at, bit_ref: (0, at))
    small = pl.BlockSpec((rows_here, rank), lambda at, bit_ref: (0, 0))
    return pl.pallas_call(
        functools.partial(low_body, part),
        grid_spec=pltpu.PrefetchScalarGridSpec(
            num_scalar_prefetch=1,
            grid=(width // step,),
            in_specs=[small, wide, small, wide],
            out_specs=(out_spec, out_spec),
            scratch_shapes=[pltpu.VMEM((rank, step), F32)],
        ),
        out_shape=(jax.ShapeDtypeStruct(shape, BF16), jax.ShapeDtypeStruct(shape, F32)),
        cost_estimate=pl.CostEstimate(
            flops=4 * rank * rows_here * width,
            bytes_accessed=width * (4 * rows_here + 6 * rank),
            transcendentals=0,
        ),
        name="low_grads",
    )(bit, backs, features, codes, cotangent)


def items_sum(send, keep, index):
    bits = lax.axis_size("items").bit_length() - 1
    came = swapped(send, "items", 0)
    for level in range(1, bits):
        mine = (index >> level) & 1
        shape = (keep.shape[0] // 2, 2, *keep.shape[1:])
        keep, came = keep.reshape(shape), came.reshape(shape)
        leave = pick(keep, 1 - mine, 1) + pick(came, 1 - mine, 1).astype(F32)
        keep = pick(keep, mine, 1) + pick(came, mine, 1).astype(F32)
        came = swapped(leave.astype(BF16), "items", level)
    return keep[0], came[0]


def share_body(share, units, unit, pos_ref, item_ref, w_ref, *refs):
    out_refs, sems = refs[:2], refs[2]
    pieces = BLOCK // unit
    copies = []
    for way in range(2):
        for one in range(units):
            number = item_ref[0] * units + one
            block = pos_ref[(2 + way) * share + lax.div(number, pieces)]
            first = pl.multiple_of(lax.rem(number, pieces) * unit, unit)
            copies.append(
                pltpu.make_async_copy(
                    w_ref.at[block, pl.ds(first, unit), :],
                    out_refs[way].at[one],
                    sems.at[way * units + one],
                )
            )
    for copy in copies:
        copy.start()
    for copy in copies:
        copy.wait()


def weight_share(block_weights, pos, item, share, unit, units):
    return pl.pallas_call(
        functools.partial(share_body, share, units, unit),
        in_specs=[
            pl.BlockSpec(memory_space=pltpu.SMEM),
            pl.BlockSpec(memory_space=pltpu.SMEM),
            pl.BlockSpec(memory_space=pl.ANY),
        ],
        out_specs=(pl.BlockSpec(memory_space=pltpu.VMEM),) * 2,
        out_shape=(jax.ShapeDtypeStruct((units, unit, BLOCK), BF16),) * 2,
        scratch_shapes=[pltpu.SemaphoreType.DMA((2 * units,))],
        cost_estimate=pl.CostEstimate(
            flops=0, bytes_accessed=8 * units * unit * BLOCK, transcendentals=0
        ),
        name="weight_share",
    )(pos, item, block_weights)


def mixed_body(share, sizes, first, last, units, unit, order, pos_ref, item_ref, f_ref, w_ref, codes_ref, low_ref, *refs):
    steps = last - first
    far_refs, refs = refs[: 2 * steps], refs[2 * steps :]
    parts = len(order)
    far_w, refs = refs[: 2 * parts], refs[2 * parts :]
    out_ref, f_buf, low_buf, far_buf, w_buf, out_buf, in_sems, w_sems, far_w_sems, out_sems = refs[-10:]
    dims = (((1,), (1,)), ((), ()))
    pieces = BLOCK // unit
    item = item_ref[0]
    starts = [sum(sizes[:one]) for one in range(len(sizes))]

    first_col, last_col = starts[first], starts[last - 1] + sizes[last - 1]
    gathered = []
    for way in range(2):
        for slot, apart in enumerate(order):
            for one in range(units):
                number = (item ^ apart) * units + one
                block, piece = lax.div(number, pieces), lax.rem(number, pieces)
                rows = pl.ds(pl.multiple_of(piece * unit, unit), unit)
                copy = pltpu.make_async_copy(
                    far_w[way * parts + slot].at[one],
                    w_buf.at[2 + way, block, rows, :],
                    far_w_sems.at[way, number],
                )
                gathered.append(((block >= first_col) & (block < last_col), copy))
    loads = []
    for step in range(steps):
        chunk = first + step
        cols = pl.ds(starts[chunk] * BLOCK, sizes[chunk] * BLOCK)
        copies = [
            pltpu.make_async_copy(f_ref.at[:, cols], f_buf.at[:, cols], in_sems.at[step, 0]),
            pltpu.make_async_copy(low_ref.at[:, cols], low_buf.at[:, cols], in_sems.at[step, 1]),
        ]
        for way in range(2):
            copies.append(
                pltpu.make_async_copy(
                    far_refs[way * steps + step], far_buf.at[way, :, cols], in_sems.at[step, 2 + way]
                )
            )
        for at in range(starts[chunk], starts[chunk] + sizes[chunk]):
            copies.append(
                pltpu.make_async_copy(w_ref.at[pos_ref[at]], w_buf.at[0, at], w_sems.at[0, at])
            )
            copies.append(
                pltpu.make_async_copy(
                    w_ref.at[pos_ref[share + (at ^ 1)]], w_buf.at[1, at], w_sems.at[1, at]
                )
            )
        loads.append(copies)
    for copy in loads[0]:
        copy.start()
    for wanted, copy in gathered:
        pl.when(wanted)(copy.start)
    for copies in loads[1:]:
        for copy in copies:
            copy.start()
    for way in range(2):
        for at in range(first_col, last_col):
            for piece in range(pieces):
                rows = pl.ds(piece * unit, unit)
                loads[[starts[one] <= at < starts[one] + sizes[one] for one in range(first, last)].index(True)].append(
                    pltpu.make_async_copy(
                        far_w[way * parts].at[0],
                        w_buf.at[2 + way, at, rows, :],
                        far_w_sems.at[way, at * pieces + piece],
                    )
                )
    stores = []
    for step in range(steps):
        chunk = first + step
        for copy in loads[step]:
            copy.wait()
        for at in range(starts[chunk], starts[chunk] + sizes[chunk]):
            own = slice(at * BLOCK, (at + 1) * BLOCK)
            flip = slice((at ^ 1) * BLOCK, ((at ^ 1) + 1) * BLOCK)
            total = lax.dot_general(f_buf[:, own], w_buf[0, at], dims, preferred_element_type=F32)
            total += lax.dot_general(f_buf[:, flip], w_buf[1, at], dims, preferred_element_type=F32)
            for way in range(2):
                total += lax.dot_general(
                    far_buf[way, :, own], w_buf[2 + way, at], dims, preferred_element_type=F32
                )
            total += jnp.dot(codes_ref[...], low_buf[:, own], preferred_element_type=F32)
            out_buf[:, own] = total.astype(BF16)
        cols = pl.ds(starts[chunk] * BLOCK, sizes[chunk] * BLOCK)
        store = pltpu.make_async_copy(out_buf.at[:, cols], out_ref.at[:, cols], out_sems.at[step])
        store.start()
        stores.append(store)
    for store in stores:
        store.wait()


def mixed_kernel(
    features, block_weights, codes, lowrank_out, far, far_weights, pos, item, sizes, first, last, units, order, held
):
    rows_here, width = features.shape
    share = width // BLOCK
    unit = far_weights[0][0].shape[1]
    hbm = pl.BlockSpec(memory_space=pltpu.HBM)
    smem = pl.BlockSpec(memory_space=pltpu.SMEM)
    far_inputs = [*far[0][first:last], *far[1][first:last], *far_weights[0], *far_weights[1]]
    inputs = [pos, item, features, block_weights, codes, lowrank_out, *far_inputs]
    if held is not None:
        inputs.append(held)
    columns = sum(sizes[first:last])
    return pl.pallas_call(
        functools.partial(mixed_body, share, sizes, first, last, units, unit, order),
        in_specs=[smem, smem, hbm, hbm, pl.BlockSpec(memory_space=pltpu.VMEM), hbm]
        + [hbm] * (len(inputs) - 6),
        out_specs=hbm,
        out_shape=jax.ShapeDtypeStruct((rows_here, width), BF16),
        input_output_aliases={} if held is None else {len(inputs) - 1: 0},
        scratch_shapes=[
            pltpu.VMEM((rows_here, width), BF16),
            pltpu.VMEM(lowrank_out.shape, BF16),
            pltpu.VMEM((2, rows_here, width), BF16),
            pltpu.VMEM((4, share, BLOCK, BLOCK), BF16),
            pltpu.VMEM((rows_here, width), BF16),
            pltpu.SemaphoreType.DMA((last - first, 4)),
            pltpu.SemaphoreType.DMA((2, share)),
            pltpu.SemaphoreType.DMA((2, len(order) * units)),
            pltpu.SemaphoreType.DMA((last - first,)),
        ],
        cost_estimate=pl.CostEstimate(
            flops=9 * columns * rows_here * BLOCK * BLOCK,
            bytes_accessed=columns * BLOCK * 2 * (4 * rows_here + 4 * BLOCK),
            transcendentals=0,
        ),
        name="mixed",
    )(*inputs)


def place_body(keys, pairs, pos_ref, *refs):
    count = len(keys) * (2 if pairs else 1)
    inputs, refs = refs[:count], refs[-(count + 4) :]
    out_ref, bufs, (rows_ref, in_sems, out_sems) = refs[0], refs[1 : 1 + count], refs[1 + count :]
    loads = [
        pltpu.make_async_copy(inputs[one], bufs[one], in_sems.at[one]) for one in range(count)
    ]
    for copy in loads:
        copy.start()
    copies = []
    per = 2 if pairs else 1
    for one, numbers in enumerate(keys):
        for copy in loads[per * one : per * (one + 1)]:
            copy.wait()
        for at, key in enumerate(numbers):
            block = bufs[per * one][at].astype(F32)
            if pairs:
                block += bufs[per * one + 1][at].astype(F32)
            slot = len(copies)
            rows_ref[slot, :, 0, :] = block
            copy = pltpu.make_async_copy(
                rows_ref.at[slot], out_ref.at[:, pl.ds(pos_ref[key], 1), :], out_sems.at[slot]
            )
            copy.start()
            copies.append(copy)
    for copy in copies:
        copy.wait()


def place_kernel(pieces, keys, pos, held, stored, pairs=False):
    part = pieces[0].shape[1]
    total = sum(len(numbers) for numbers in keys)
    hbm = pl.BlockSpec(memory_space=pltpu.HBM)
    inputs = [pos, *pieces] + ([] if held is None else [held])
    return pl.pallas_call(
        functools.partial(place_body, keys, pairs),
        in_specs=[pl.BlockSpec(memory_space=pltpu.SMEM)] + [hbm] * (len(inputs) - 1),
        out_specs=hbm,
        out_shape=jax.ShapeDtypeStruct((part, stored, BLOCK), F32),
        input_output_aliases={} if held is None else {len(inputs) - 1: 0},
        scratch_shapes=[pltpu.VMEM(piece.shape, piece.dtype) for piece in pieces]
        + [
            pltpu.VMEM((total, part, 1, BLOCK), F32),
            pltpu.SemaphoreType.DMA((len(pieces),)),
            pltpu.SemaphoreType.DMA((total,)),
        ],
        cost_estimate=pl.CostEstimate(
            flops=0, bytes_accessed=8 * total * part * BLOCK, transcendentals=0
        ),
        name="place",
    )(*inputs)


def layer(features, cotangent, block_weights, block_rows, block_cols, lowrank_in, lowrank_out):
    _, width = features.shape
    share = width // BLOCK
    count = WIDTH // BLOCK
    stored = block_weights.shape[0]
    sizes = chunk_sizes(share)
    chunks = len(sizes)
    items = lax.axis_size("items")
    item = lax.axis_index("items").astype(jnp.int32)
    item_arg = item.reshape(1)
    bits = items.bit_length() - 1
    place = lax.axis_index("wloop")
    way_bits = lax.axis_size("wloop").bit_length() - 1
    far_bits = (way_bits - 2, way_bits - 1)

    def hop(value, bit):
        return swapped(value, "wloop", bit)

    stride_of = jnp.bitwise_xor(block_rows, block_cols)
    stride_id = (stride_of == 1) * 1 + (stride_of == count // 4) * 2 + (stride_of == count // 2) * 3
    key = stride_id * share + block_cols % share
    pos = jnp.sum(
        jnp.where(
            key[None, :] == jnp.arange(4 * share, dtype=jnp.int32)[:, None],
            jnp.arange(stored, dtype=jnp.int32)[None, :],
            0,
        ),
        axis=1,
    ).astype(jnp.int32)

    far, source = [[], []], features
    for one in range(chunks):
        first = sum(sizes[:one]) * BLOCK
        piece = source[:, first : first + sizes[one] * BLOCK]
        if one + 1 < chunks:
            source = after(source, piece)
        for way in range(2):
            far[way].append(hop(piece, far_bits[way]))

    unit = min(BLOCK, share * BLOCK // items)
    units = share * BLOCK // items // unit
    shares = weight_share(block_weights, pos, item_arg, share, unit, units)
    far_weights, order = [], []
    for way in range(2):
        held, order = [hop(shares[way], far_bits[way])], [0]
        for level in range(bits - 1, -1, -1):
            for one in range(len(held)):
                held.append(swapped(held[one], "items", level))
                order.append(order[one] ^ (1 << level))
        far_weights.append(held)

    dims = (((1,), (1,)), ((), ()))
    codes = jnp.stack(
        [
            lax.dot_general(features, lowrank_in, dims, preferred_element_type=F32),
            lax.dot_general(cotangent, lowrank_out, dims, preferred_element_type=F32),
        ]
    )
    for level in range(way_bits - 1):
        mine = (place >> level) & 1
        split = codes.reshape(2, 2, codes.shape[1] // 2, codes.shape[2])
        codes = pick(split, mine, 1) + hop(pick(split, 1 - mine, 1), level)
    came = hop(codes, way_bits - 1)
    codes = (codes + came).astype(BF16)
    for level in range(way_bits - 2, -1, -1):
        mine = (place >> level) & 1
        other = hop(codes, level)
        codes = jnp.where(
            mine == 0,
            jnp.concatenate([codes, other], axis=1),
            jnp.concatenate([other, codes], axis=1),
        )
    codes, backs = codes[0], codes[1]

    bit = item_arg & 1
    own = pair_grads(bit, cotangent, [features], ((0, 0), (0, 1)), 0, share, items)
    own = items_sum(*own, item)
    block_grads = place_kernel(
        [part for way in range(2) for part in (own[0][way], own[1][way])],
        [list(range(way * share, (way + 1) * share)) for way in range(2)],
        pos,
        None,
        stored,
        pairs=True,
    )
    returned = [[], []]
    for one in range(chunks):
        pairs = pair_grads(
            bit,
            cotangent,
            [far[0][one], far[1][one]],
            ((0, 0), (1, 0)),
            sum(sizes[:one]),
            sizes[one],
            items,
        )
        keep, came = items_sum(*pairs, item)
        for way in range(2):
            done = (keep[way] + came[way].astype(F32)).astype(BF16)
            returned[way].append(hop(done, far_bits[way]))

    low = low_kernel(bit, backs, features, codes, cotangent, items)
    keep, came = items_sum(*low, item)
    low = [keep[way] + came[way].astype(F32) for way in range(2)]

    mixed = None
    early = min(EARLY_CHUNKS, chunks - 1)
    for first, last in ((0, early), (early, chunks)):
        mixed = mixed_kernel(
            features,
            block_weights,
            codes,
            lowrank_out,
            far,
            far_weights,
            pos,
            item_arg,
            sizes,
            first,
            last,
            units,
            order,
            mixed,
        )
    for first, last in ((0, chunks - 1), (chunks - 1, chunks)):
        pieces, keys = [], []
        for way in range(2):
            for one in range(first, last):
                start = (2 + way) * share + sum(sizes[:one])
                pieces.append(returned[way][one])
                keys.append(list(range(start, start + sizes[one])))
        block_grads = place_kernel(pieces, keys, pos, block_grads, stored)
    return (mixed, block_grads, low[0], low[1])


def chunk_sizes(share):
    return CHUNK_SIZES if sum(CHUNK_SIZES) == share else (1,) * share


def solution(mesh):
    return jax.shard_map(
        layer,
        mesh=mesh,
        in_specs=(
            P(("groups", "items"), "wloop"),
            P(("groups", "items"), "wloop"),
            P("wloop", None, None),
            P("wloop"),
            P("wloop"),
            P(None, "wloop"),
            P(None, "wloop"),
        ),
        out_specs=(
            P(("groups", "items"), "wloop"),
            P(("groups", "items"), "wloop", None),
            P(("groups", "items"), "wloop"),
            P(("groups", "items"), "wloop"),
        ),
        check_vma=False,
    )
```

```python
import functools

import jax
import jax.numpy as jnp
from jax import lax
from jax.experimental import pallas as pl
from jax.experimental.pallas import tpu as pltpu
from jax.sharding import PartitionSpec as P


WIDTH = 16384
BLOCK = 256
VMEM_LIMIT = 67_043_328
CHUNK_SIZES = (6, 6, 4)
EARLY_CHUNKS = 2


F32 = jnp.float32
BF16 = jnp.bfloat16


def swapped(block, axis, apart):
    count = lax.axis_size(axis)
    return lax.ppermute(block, axis, [(one, one ^ (1 << apart)) for one in range(count)])


def after(value, *deps):
    return lax.optimization_barrier((value, *deps))[0]


def pick(values, index, dim):
    return lax.dynamic_index_in_dim(values, index, dim, keepdims=False)


def grad_body(pairs, part, first, step, bit_ref, g_ref, *refs):
    count = (len(refs) - 7) // 2
    f_refs, (send_ref, keep_ref, g_buf), refs = refs[:count], refs[count : count + 3], refs[count + 3 :]
    f_bufs, (send_buf, keep_buf, in_sems, out_sems) = refs[:count], refs[count:]
    bit = bit_ref[0]
    groups = g_buf.shape[1] // (step * BLOCK)
    halves = send_ref.shape[0]
    loads = []
    for group in range(groups):
        cols = pl.ds(group * step * BLOCK, step * BLOCK)
        there = pl.ds((first + group * step) * BLOCK, step * BLOCK)
        loads.append(
            [pltpu.make_async_copy(g_ref.at[:, there], g_buf.at[:, cols], in_sems.at[group, 0])]
            + [
                pltpu.make_async_copy(
                    f_refs[one].at[:, cols], f_bufs[one].at[:, cols], in_sems.at[group, 1 + one]
                )
                for one in range(count)
            ]
        )
    for copies in loads:
        for copy in copies:
            copy.start()
    stores = []
    for group in range(groups):
        for copy in loads[group]:
            copy.wait()
        for at in range(group * step, (group + 1) * step):
            for slot, (f_at, flip) in enumerate(pairs):
                g_at = at ^ flip
                total = lax.dot_general(
                    g_buf[:, g_at * BLOCK : (g_at + 1) * BLOCK],
                    f_bufs[f_at][:, at * BLOCK : (at + 1) * BLOCK],
                    (((0,), (0,)), ((), ())),
                    preferred_element_type=F32,
                )
                for half in range(halves):
                    low = total[2 * half * part : (2 * half + 1) * part]
                    high = total[(2 * half + 1) * part : (2 * half + 2) * part]
                    keep_buf[half, slot, at] = jnp.where(bit == 0, low, high)
                    send_buf[half, slot, at] = jnp.where(bit == 0, high, low).astype(BF16)
        span = pl.ds(group * step, step)
        for which, (buf, ref) in enumerate(((send_buf, send_ref), (keep_buf, keep_ref))):
            copy = pltpu.make_async_copy(
                buf.at[:, :, span], ref.at[:, :, span], out_sems.at[group, which]
            )
            copy.start()
            stores.append(copy)
    for copy in stores:
        copy.wait()


def pair_grads(bit, cotangent, features, pairs, first, count, parts):
    rows_here = cotangent.shape[0]
    part = BLOCK // parts
    step = 2 if count % 2 == 0 else 1
    shape = (parts // 2, 2, count, part, BLOCK)
    wide = pltpu.VMEM((rows_here, count * BLOCK), BF16)
    hbm = pl.BlockSpec(memory_space=pltpu.HBM)
    return pl.pallas_call(
        functools.partial(grad_body, pairs, part, first, step),
        in_specs=[pl.BlockSpec(memory_space=pltpu.SMEM)] + [hbm] * (1 + len(features)),
        out_specs=(hbm, hbm),
        scratch_shapes=[wide] * (1 + len(features))
        + [
            pltpu.VMEM(shape, BF16),
            pltpu.VMEM(shape, F32),
            pltpu.SemaphoreType.DMA((count // step, 1 + len(features))),
            pltpu.SemaphoreType.DMA((count // step, 2)),
        ],
        out_shape=(jax.ShapeDtypeStruct(shape, BF16), jax.ShapeDtypeStruct(shape, F32)),
        compiler_params=pltpu.CompilerParams(vmem_limit_bytes=VMEM_LIMIT),
        cost_estimate=pl.CostEstimate(
            flops=4 * count * rows_here * BLOCK * BLOCK,
            bytes_accessed=count * BLOCK * (2 * rows_here * 3 + 6 * BLOCK),
            transcendentals=0,
        ),
        name="pair_grads",
    )(bit, cotangent, *features)


def low_body(part, bit_ref, b_ref, f_ref, c_ref, g_ref, send_ref, keep_ref, acc_ref):
    bit = bit_ref[0]
    for slot, (small, wide) in enumerate(((b_ref, f_ref), (c_ref, g_ref))):
        acc_ref[...] = lax.dot_general(
            small[...], wide[...], (((0,), (0,)), ((), ())), preferred_element_type=F32
        )
        for half in range(send_ref.shape[0]):
            first = pl.multiple_of((2 * half + bit) * part, part)
            other = pl.multiple_of((2 * half + 1 - bit) * part, part)
            keep_ref[half, slot] = acc_ref[pl.ds(first, part), :]
            send_ref[half, slot] = acc_ref[pl.ds(other, part), :].astype(BF16)


def low_kernel(bit, backs, features, codes, cotangent, parts):
    rows_here, width = features.shape
    rank = codes.shape[1]
    part = rank // parts
    step = min(1024, width)
    out_spec = pl.BlockSpec((parts // 2, 2, part, step), lambda at, bit_ref: (0, 0, 0, at))
    shape = (parts // 2, 2, part, width)
    wide = pl.BlockSpec((rows_here, step), lambda at, bit_ref: (0, at))
    small = pl.BlockSpec((rows_here, rank), lambda at, bit_ref: (0, 0))
    return pl.pallas_call(
        functools.partial(low_body, part),
        grid_spec=pltpu.PrefetchScalarGridSpec(
            num_scalar_prefetch=1,
            grid=(width // step,),
            in_specs=[small, wide, small, wide],
            out_specs=(out_spec, out_spec),
            scratch_shapes=[pltpu.VMEM((rank, step), F32)],
        ),
        out_shape=(jax.ShapeDtypeStruct(shape, BF16), jax.ShapeDtypeStruct(shape, F32)),
        compiler_params=pltpu.CompilerParams(vmem_limit_bytes=VMEM_LIMIT),
        cost_estimate=pl.CostEstimate(
            flops=4 * rank * rows_here * width,
            bytes_accessed=width * (4 * rows_here + 6 * rank),
            transcendentals=0,
        ),
        name="low_grads",
    )(bit, backs, features, codes, cotangent)


def items_sum(send, keep, index):
    bits = lax.axis_size("items").bit_length() - 1
    came = swapped(send, "items", 0)
    for level in range(1, bits):
        mine = (index >> level) & 1
        shape = (keep.shape[0] // 2, 2, *keep.shape[1:])
        keep, came = keep.reshape(shape), came.reshape(shape)
        leave = pick(keep, 1 - mine, 1) + pick(came, 1 - mine, 1).astype(F32)
        keep = pick(keep, mine, 1) + pick(came, mine, 1).astype(F32)
        came = swapped(leave.astype(BF16), "items", level)
    return keep[0], came[0]


def share_body(share, units, unit, pos_ref, item_ref, w_ref, *refs):
    out_refs, sems = refs[:2], refs[2]
    pieces = BLOCK // unit
    copies = []
    for way in range(2):
        for one in range(units):
            number = item_ref[0] * units + one
            block = pos_ref[(2 + way) * share + lax.div(number, pieces)]
            first = pl.multiple_of(lax.rem(number, pieces) * unit, unit)
            copies.append(
                pltpu.make_async_copy(
                    w_ref.at[block, pl.ds(first, unit), :],
                    out_refs[way].at[one],
                    sems.at[way * units + one],
                )
            )
    for copy in copies:
        copy.start()
    for copy in copies:
        copy.wait()


def weight_share(block_weights, pos, item, share, unit, units):
    return pl.pallas_call(
        functools.partial(share_body, share, units, unit),
        in_specs=[
            pl.BlockSpec(memory_space=pltpu.SMEM),
            pl.BlockSpec(memory_space=pltpu.SMEM),
            pl.BlockSpec(memory_space=pl.ANY),
        ],
        out_specs=(pl.BlockSpec(memory_space=pltpu.VMEM),) * 2,
        out_shape=(jax.ShapeDtypeStruct((units, unit, BLOCK), BF16),) * 2,
        scratch_shapes=[pltpu.SemaphoreType.DMA((2 * units,))],
        compiler_params=pltpu.CompilerParams(vmem_limit_bytes=VMEM_LIMIT),
        cost_estimate=pl.CostEstimate(
            flops=0, bytes_accessed=8 * units * unit * BLOCK, transcendentals=0
        ),
        name="weight_share",
    )(pos, item, block_weights)


def mixed_body(share, sizes, first, last, units, unit, order, pos_ref, item_ref, f_ref, w_ref, codes_ref, low_ref, *refs):
    steps = last - first
    far_refs, refs = refs[: 2 * steps], refs[2 * steps :]
    parts = len(order)
    far_w, refs = refs[:parts], refs[parts:]
    out_ref, f_buf, low_buf, far_buf, w_buf, out_buf, in_sems, w_sems, far_w_sems, out_sems = refs[-10:]
    dims = (((1,), (1,)), ((), ()))
    pieces = BLOCK // unit
    item = item_ref[0]
    starts = [sum(sizes[:one]) for one in range(len(sizes))]

    first_col, last_col = starts[first], starts[last - 1] + sizes[last - 1]
    gathered = []
    for way in range(2):
        for slot, apart in enumerate(order):
            for one in range(units):
                number = (item ^ apart) * units + one
                block, piece = lax.div(number, pieces), lax.rem(number, pieces)
                rows = pl.ds(pl.multiple_of(piece * unit, unit), unit)
                copy = pltpu.make_async_copy(
                    far_w[slot].at[way, one],
                    w_buf.at[2 + way, block, rows, :],
                    far_w_sems.at[way, number],
                )
                gathered.append(((block >= first_col) & (block < last_col), copy))
    loads = []
    for step in range(steps):
        chunk = first + step
        cols = pl.ds(starts[chunk] * BLOCK, sizes[chunk] * BLOCK)
        copies = [
            pltpu.make_async_copy(f_ref.at[:, cols], f_buf.at[:, cols], in_sems.at[step, 0]),
            pltpu.make_async_copy(low_ref.at[:, cols], low_buf.at[:, cols], in_sems.at[step, 1]),
        ]
        for way in range(2):
            copies.append(
                pltpu.make_async_copy(
                    far_refs[way * steps + step], far_buf.at[way, :, cols], in_sems.at[step, 2 + way]
                )
            )
        for at in range(starts[chunk], starts[chunk] + sizes[chunk]):
            copies.append(
                pltpu.make_async_copy(w_ref.at[pos_ref[at]], w_buf.at[0, at], w_sems.at[0, at])
            )
            copies.append(
                pltpu.make_async_copy(
                    w_ref.at[pos_ref[share + (at ^ 1)]], w_buf.at[1, at], w_sems.at[1, at]
                )
            )
        loads.append(copies)
    for copy in loads[0]:
        copy.start()
    for wanted, copy in gathered:
        pl.when(wanted)(copy.start)
    for copies in loads[1:]:
        for copy in copies:
            copy.start()
    for way in range(2):
        for at in range(first_col, last_col):
            for piece in range(pieces):
                rows = pl.ds(piece * unit, unit)
                loads[[starts[one] <= at < starts[one] + sizes[one] for one in range(first, last)].index(True)].append(
                    pltpu.make_async_copy(
                        far_w[0].at[way, 0],
                        w_buf.at[2 + way, at, rows, :],
                        far_w_sems.at[way, at * pieces + piece],
                    )
                )
    stores = []
    for step in range(steps):
        chunk = first + step
        for copy in loads[step]:
            copy.wait()
        for at in range(starts[chunk], starts[chunk] + sizes[chunk]):
            own = slice(at * BLOCK, (at + 1) * BLOCK)
            flip = slice((at ^ 1) * BLOCK, ((at ^ 1) + 1) * BLOCK)
            total = lax.dot_general(f_buf[:, own], w_buf[0, at], dims, preferred_element_type=F32)
            total += lax.dot_general(f_buf[:, flip], w_buf[1, at], dims, preferred_element_type=F32)
            for way in range(2):
                total += lax.dot_general(
                    far_buf[way, :, own], w_buf[2 + way, at], dims, preferred_element_type=F32
                )
            total += jnp.dot(codes_ref[...], low_buf[:, own], preferred_element_type=F32)
            out_buf[:, own] = total.astype(BF16)
        cols = pl.ds(starts[chunk] * BLOCK, sizes[chunk] * BLOCK)
        store = pltpu.make_async_copy(out_buf.at[:, cols], out_ref.at[:, cols], out_sems.at[step])
        store.start()
        stores.append(store)
    for store in stores:
        store.wait()


def mixed_kernel(
    features, block_weights, codes, lowrank_out, far, far_weights, pos, item, sizes, first, last, units, order, held
):
    rows_here, width = features.shape
    share = width // BLOCK
    unit = far_weights[0].shape[2]
    hbm = pl.BlockSpec(memory_space=pltpu.HBM)
    smem = pl.BlockSpec(memory_space=pltpu.SMEM)
    far_inputs = [*far[0][first:last], *far[1][first:last], *far_weights]
    inputs = [pos, item, features, block_weights, codes, lowrank_out, *far_inputs]
    if held is not None:
        inputs.append(held)
    columns = sum(sizes[first:last])
    return pl.pallas_call(
        functools.partial(mixed_body, share, sizes, first, last, units, unit, order),
        in_specs=[smem, smem, hbm, hbm, pl.BlockSpec(memory_space=pltpu.VMEM), hbm]
        + [hbm] * (len(inputs) - 6),
        out_specs=hbm,
        out_shape=jax.ShapeDtypeStruct((rows_here, width), BF16),
        input_output_aliases={} if held is None else {len(inputs) - 1: 0},
        scratch_shapes=[
            pltpu.VMEM((rows_here, width), BF16),
            pltpu.VMEM(lowrank_out.shape, BF16),
            pltpu.VMEM((2, rows_here, width), BF16),
            pltpu.VMEM((4, share, BLOCK, BLOCK), BF16),
            pltpu.VMEM((rows_here, width), BF16),
            pltpu.SemaphoreType.DMA((last - first, 4)),
            pltpu.SemaphoreType.DMA((2, share)),
            pltpu.SemaphoreType.DMA((2, len(order) * units)),
            pltpu.SemaphoreType.DMA((last - first,)),
        ],
        compiler_params=pltpu.CompilerParams(vmem_limit_bytes=VMEM_LIMIT),
        cost_estimate=pl.CostEstimate(
            flops=9 * columns * rows_here * BLOCK * BLOCK,
            bytes_accessed=columns * BLOCK * 2 * (4 * rows_here + 4 * BLOCK),
            transcendentals=0,
        ),
        name="mixed",
    )(*inputs)


def place_body(keys, pairs, pos_ref, *refs):
    count = len(keys) * (2 if pairs else 1)
    inputs, refs = refs[:count], refs[-(count + 4) :]
    out_ref, bufs, (rows_ref, in_sems, out_sems) = refs[0], refs[1 : 1 + count], refs[1 + count :]
    loads = [
        pltpu.make_async_copy(inputs[one], bufs[one], in_sems.at[one]) for one in range(count)
    ]
    for copy in loads:
        copy.start()
    copies = []
    per = 2 if pairs else 1
    for one, numbers in enumerate(keys):
        for copy in loads[per * one : per * (one + 1)]:
            copy.wait()
        for at, key in enumerate(numbers):
            block = bufs[per * one][at].astype(F32)
            if pairs:
                block += bufs[per * one + 1][at].astype(F32)
            slot = len(copies)
            rows_ref[slot, :, 0, :] = block
            copy = pltpu.make_async_copy(
                rows_ref.at[slot], out_ref.at[:, pl.ds(pos_ref[key], 1), :], out_sems.at[slot]
            )
            copy.start()
            copies.append(copy)
    for copy in copies:
        copy.wait()


def place_kernel(pieces, keys, pos, held, stored, pairs=False):
    part = pieces[0].shape[1]
    total = sum(len(numbers) for numbers in keys)
    hbm = pl.BlockSpec(memory_space=pltpu.HBM)
    inputs = [pos, *pieces] + ([] if held is None else [held])
    return pl.pallas_call(
        functools.partial(place_body, keys, pairs),
        in_specs=[pl.BlockSpec(memory_space=pltpu.SMEM)] + [hbm] * (len(inputs) - 1),
        out_specs=hbm,
        out_shape=jax.ShapeDtypeStruct((part, stored, BLOCK), F32),
        input_output_aliases={} if held is None else {len(inputs) - 1: 0},
        scratch_shapes=[pltpu.VMEM(piece.shape, piece.dtype) for piece in pieces]
        + [
            pltpu.VMEM((total, part, 1, BLOCK), F32),
            pltpu.SemaphoreType.DMA((len(pieces),)),
            pltpu.SemaphoreType.DMA((total,)),
        ],
        compiler_params=pltpu.CompilerParams(vmem_limit_bytes=VMEM_LIMIT),
        cost_estimate=pl.CostEstimate(
            flops=0, bytes_accessed=8 * total * part * BLOCK, transcendentals=0
        ),
        name="place",
    )(*inputs)


def layer(features, cotangent, block_weights, block_rows, block_cols, lowrank_in, lowrank_out):
    _, width = features.shape
    share = width // BLOCK
    count = WIDTH // BLOCK
    stored = block_weights.shape[0]
    sizes = chunk_sizes(share)
    chunks = len(sizes)
    items = lax.axis_size("items")
    item = lax.axis_index("items").astype(jnp.int32)
    item_arg = item.reshape(1)
    groups = lax.axis_size("groups")
    sharer = (lax.axis_index("groups").astype(jnp.int32) * items + item).reshape(1)
    sharers = groups * items
    part = BLOCK // items
    bits = items.bit_length() - 1
    place = lax.axis_index("wloop")
    way_bits = lax.axis_size("wloop").bit_length() - 1
    far_bits = (way_bits - 2, way_bits - 1)

    def hop(value, bit):
        return swapped(value, "wloop", bit)

    stride_of = jnp.bitwise_xor(block_rows, block_cols)
    stride_id = (stride_of == 1) * 1 + (stride_of == count // 4) * 2 + (stride_of == count // 2) * 3
    key = stride_id * share + block_cols % share
    pos = jnp.sum(
        jnp.where(
            key[None, :] == jnp.arange(4 * share, dtype=jnp.int32)[:, None],
            jnp.arange(stored, dtype=jnp.int32)[None, :],
            0,
        ),
        axis=1,
    ).astype(jnp.int32)

    far, source = [[], []], features
    for one in range(chunks):
        first = sum(sizes[:one]) * BLOCK
        piece = source[:, first : first + sizes[one] * BLOCK]
        if one + 1 < chunks:
            source = after(source, piece)
        for way in range(2):
            far[way].append(hop(piece, far_bits[way]))

    unit = min(BLOCK, share * BLOCK // sharers)
    units = share * BLOCK // sharers // unit
    shares = weight_share(block_weights, pos, sharer, share, unit, units)
    held = [hop(shares[way], far_bits[way]) for way in range(2)]
    far_weights, order = [jnp.stack(held)], [0]
    hops = [("items", level, 1 << level) for level in range(bits - 1, 0, -1)]
    hops += [("groups", level, items << level) for level in range(groups.bit_length() - 1)]
    hops += [("items", 0, 1)]
    for axis, level, apart in hops:
        for one in range(len(order)):
            far_weights.append(swapped(far_weights[one], axis, level))
            order.append(order[one] ^ apart)

    dims = (((1,), (1,)), ((), ()))
    codes = jnp.stack(
        [
            lax.dot_general(features, lowrank_in, dims, preferred_element_type=F32),
            lax.dot_general(cotangent, lowrank_out, dims, preferred_element_type=F32),
        ]
    )
    for level in range(way_bits - 1):
        mine = (place >> level) & 1
        split = codes.reshape(2, 2, codes.shape[1] // 2, codes.shape[2])
        codes = pick(split, mine, 1) + hop(pick(split, 1 - mine, 1), level)
    came = hop(codes, way_bits - 1)
    codes = (codes + came).astype(BF16)
    for level in range(way_bits - 2, -1, -1):
        mine = (place >> level) & 1
        other = hop(codes, level)
        codes = jnp.where(
            mine == 0,
            jnp.concatenate([codes, other], axis=1),
            jnp.concatenate([other, codes], axis=1),
        )
    codes, backs = codes[0], codes[1]

    bit = item_arg & 1
    own = pair_grads(bit, cotangent, [features], ((0, 0), (0, 1)), 0, share, items)
    own = items_sum(*own, item)
    shape = (2 * share, part, BLOCK)
    block_grads = place_kernel(
        [own[0].reshape(shape), own[1].reshape(shape)],
        [list(range(2 * share))],
        pos,
        None,
        stored,
        pairs=True,
    )
    returned = [[], []]
    for one in range(chunks):
        pairs = pair_grads(
            bit,
            cotangent,
            [far[0][one], far[1][one]],
            ((0, 0), (1, 0)),
            sum(sizes[:one]),
            sizes[one],
            items,
        )
        keep, came = items_sum(*pairs, item)
        for way in range(2):
            done = (keep[way] + came[way].astype(F32)).astype(BF16)
            returned[way].append(hop(done, far_bits[way]))

    low = low_kernel(bit, backs, features, codes, cotangent, items)
    keep, came = items_sum(*low, item)
    low = [keep[way] + came[way].astype(F32) for way in range(2)]

    mixed = None
    early = min(EARLY_CHUNKS, chunks - 1)
    for first, last in ((0, early), (early, chunks)):
        mixed = mixed_kernel(
            features,
            block_weights,
            codes,
            lowrank_out,
            far,
            far_weights,
            pos,
            sharer,
            sizes,
            first,
            last,
            units,
            order,
            mixed,
        )
    for first, last in ((0, chunks - 1), (chunks - 1, chunks)):
        pieces, keys = [], []
        for way in range(2):
            for one in range(first, last):
                start = (2 + way) * share + sum(sizes[:one])
                pieces.append(returned[way][one])
                keys.append(list(range(start, start + sizes[one])))
        block_grads = place_kernel(pieces, keys, pos, block_grads, stored)
    return (mixed, block_grads, low[0], low[1])


def chunk_sizes(share):
    return CHUNK_SIZES if sum(CHUNK_SIZES) == share else (1,) * share


def solution(mesh):
    return jax.shard_map(
        layer,
        mesh=mesh,
        in_specs=(
            P(("groups", "items"), "wloop"),
            P(("groups", "items"), "wloop"),
            P("wloop", None, None),
            P("wloop"),
            P("wloop"),
            P(None, "wloop"),
            P(None, "wloop"),
        ),
        out_specs=(
            P(("groups", "items"), "wloop"),
            P(("groups", "items"), "wloop", None),
            P(("groups", "items"), "wloop"),
            P(("groups", "items"), "wloop"),
        ),
        check_vma=False,
    )
```

```python
import functools

import jax
import jax.numpy as jnp
from jax import lax
from jax.experimental import pallas as pl
from jax.experimental.pallas import tpu as pltpu
from jax.sharding import PartitionSpec as P


WIDTH = 16384
BLOCK = 256
VMEM_LIMIT = 67_043_328
CHUNK_SIZES = (4, 4, 5, 3)


F32 = jnp.float32
BF16 = jnp.bfloat16


def swapped(block, axis, apart):
    count = lax.axis_size(axis)
    return lax.ppermute(block, axis, [(one, one ^ (1 << apart)) for one in range(count)])


def after(value, *deps):
    return lax.optimization_barrier((value, *deps))[0]


def pick(values, index, dim):
    return lax.dynamic_index_in_dim(values, index, dim, keepdims=False)


def grad_body(pairs, part, first, step, bit_ref, g_ref, *refs):
    count = (len(refs) - 7) // 2
    f_refs, (send_ref, keep_ref, g_buf), refs = refs[:count], refs[count : count + 3], refs[count + 3 :]
    f_bufs, (send_buf, keep_buf, in_sems, out_sems) = refs[:count], refs[count:]
    bit = bit_ref[0]
    groups = g_buf.shape[1] // (step * BLOCK)
    halves = send_ref.shape[0]
    loads = []
    for group in range(groups):
        cols = pl.ds(group * step * BLOCK, step * BLOCK)
        there = pl.ds((first + group * step) * BLOCK, step * BLOCK)
        loads.append(
            [pltpu.make_async_copy(g_ref.at[:, there], g_buf.at[:, cols], in_sems.at[group, 0])]
            + [
                pltpu.make_async_copy(
                    f_refs[one].at[:, cols], f_bufs[one].at[:, cols], in_sems.at[group, 1 + one]
                )
                for one in range(count)
            ]
        )
    for copies in loads:
        for copy in copies:
            copy.start()
    stores = []
    for group in range(groups):
        for copy in loads[group]:
            copy.wait()
        for at in range(group * step, (group + 1) * step):
            for slot, (f_at, flip) in enumerate(pairs):
                g_at = at ^ flip
                total = lax.dot_general(
                    g_buf[:, g_at * BLOCK : (g_at + 1) * BLOCK],
                    f_bufs[f_at][:, at * BLOCK : (at + 1) * BLOCK],
                    (((0,), (0,)), ((), ())),
                    preferred_element_type=F32,
                )
                for half in range(halves):
                    low = total[2 * half * part : (2 * half + 1) * part]
                    high = total[(2 * half + 1) * part : (2 * half + 2) * part]
                    keep_buf[half, slot, at] = jnp.where(bit == 0, low, high)
                    send_buf[half, slot, at] = jnp.where(bit == 0, high, low).astype(BF16)
        span = pl.ds(group * step, step)
        for which, (buf, ref) in enumerate(((send_buf, send_ref), (keep_buf, keep_ref))):
            copy = pltpu.make_async_copy(
                buf.at[:, :, span], ref.at[:, :, span], out_sems.at[group, which]
            )
            copy.start()
            stores.append(copy)
    for copy in stores:
        copy.wait()


def pair_grads(bit, cotangent, features, pairs, first, count, parts):
    rows_here = cotangent.shape[0]
    part = BLOCK // parts
    step = 2 if count % 2 == 0 else 1
    shape = (parts // 2, 2, count, part, BLOCK)
    wide = pltpu.VMEM((rows_here, count * BLOCK), BF16)
    hbm = pl.BlockSpec(memory_space=pltpu.HBM)
    return pl.pallas_call(
        functools.partial(grad_body, pairs, part, first, step),
        in_specs=[pl.BlockSpec(memory_space=pltpu.SMEM)] + [hbm] * (1 + len(features)),
        out_specs=(hbm, hbm),
        scratch_shapes=[wide] * (1 + len(features))
        + [
            pltpu.VMEM(shape, BF16),
            pltpu.VMEM(shape, F32),
            pltpu.SemaphoreType.DMA((count // step, 1 + len(features))),
            pltpu.SemaphoreType.DMA((count // step, 2)),
        ],
        out_shape=(jax.ShapeDtypeStruct(shape, BF16), jax.ShapeDtypeStruct(shape, F32)),
        compiler_params=pltpu.CompilerParams(vmem_limit_bytes=VMEM_LIMIT),
        cost_estimate=pl.CostEstimate(
            flops=4 * count * rows_here * BLOCK * BLOCK,
            bytes_accessed=count * BLOCK * (2 * rows_here * 3 + 6 * BLOCK),
            transcendentals=0,
        ),
        name="pair_grads",
    )(bit, cotangent, *features)


def low_body(part, bit_ref, b_ref, f_ref, c_ref, g_ref, send_ref, keep_ref, acc_ref):
    bit = bit_ref[0]
    for slot, (small, wide) in enumerate(((b_ref, f_ref), (c_ref, g_ref))):
        acc_ref[...] = lax.dot_general(
            small[...], wide[...], (((0,), (0,)), ((), ())), preferred_element_type=F32
        )
        for half in range(send_ref.shape[0]):
            first = pl.multiple_of((2 * half + bit) * part, part)
            other = pl.multiple_of((2 * half + 1 - bit) * part, part)
            keep_ref[half, slot] = acc_ref[pl.ds(first, part), :]
            send_ref[half, slot] = acc_ref[pl.ds(other, part), :].astype(BF16)


def low_kernel(bit, backs, features, codes, cotangent, parts):
    rows_here, width = features.shape
    rank = codes.shape[1]
    part = rank // parts
    step = min(1024, width)
    out_spec = pl.BlockSpec((parts // 2, 2, part, step), lambda at, bit_ref: (0, 0, 0, at))
    shape = (parts // 2, 2, part, width)
    wide = pl.BlockSpec((rows_here, step), lambda at, bit_ref: (0, at))
    small = pl.BlockSpec((rows_here, rank), lambda at, bit_ref: (0, 0))
    return pl.pallas_call(
        functools.partial(low_body, part),
        grid_spec=pltpu.PrefetchScalarGridSpec(
            num_scalar_prefetch=1,
            grid=(width // step,),
            in_specs=[small, wide, small, wide],
            out_specs=(out_spec, out_spec),
            scratch_shapes=[pltpu.VMEM((rank, step), F32)],
        ),
        out_shape=(jax.ShapeDtypeStruct(shape, BF16), jax.ShapeDtypeStruct(shape, F32)),
        compiler_params=pltpu.CompilerParams(vmem_limit_bytes=VMEM_LIMIT),
        cost_estimate=pl.CostEstimate(
            flops=4 * rank * rows_here * width,
            bytes_accessed=width * (4 * rows_here + 6 * rank),
            transcendentals=0,
        ),
        name="low_grads",
    )(bit, backs, features, codes, cotangent)


def items_sum(send, keep, index):
    bits = lax.axis_size("items").bit_length() - 1
    came = swapped(send, "items", 0)
    for level in range(1, bits):
        mine = (index >> level) & 1
        shape = (keep.shape[0] // 2, 2, *keep.shape[1:])
        keep, came = keep.reshape(shape), came.reshape(shape)
        leave = pick(keep, 1 - mine, 1) + pick(came, 1 - mine, 1).astype(F32)
        keep = pick(keep, mine, 1) + pick(came, mine, 1).astype(F32)
        came = swapped(leave.astype(BF16), "items", level)
    return keep[0], came[0]


def share_body(share, units, unit, pos_ref, item_ref, w_ref, *refs):
    out_refs, sems = refs[:2], refs[2]
    pieces = BLOCK // unit
    copies = []
    for way in range(2):
        for one in range(units):
            number = item_ref[0] * units + one
            block = pos_ref[(2 + way) * share + lax.div(number, pieces)]
            first = pl.multiple_of(lax.rem(number, pieces) * unit, unit)
            copies.append(
                pltpu.make_async_copy(
                    w_ref.at[block, pl.ds(first, unit), :],
                    out_refs[way].at[one],
                    sems.at[way * units + one],
                )
            )
    for copy in copies:
        copy.start()
    for copy in copies:
        copy.wait()


def weight_share(block_weights, pos, item, share, unit, units):
    return pl.pallas_call(
        functools.partial(share_body, share, units, unit),
        in_specs=[
            pl.BlockSpec(memory_space=pltpu.SMEM),
            pl.BlockSpec(memory_space=pltpu.SMEM),
            pl.BlockSpec(memory_space=pl.ANY),
        ],
        out_specs=(pl.BlockSpec(memory_space=pltpu.VMEM),) * 2,
        out_shape=(jax.ShapeDtypeStruct((units, unit, BLOCK), BF16),) * 2,
        scratch_shapes=[pltpu.SemaphoreType.DMA((2 * units,))],
        compiler_params=pltpu.CompilerParams(vmem_limit_bytes=VMEM_LIMIT),
        cost_estimate=pl.CostEstimate(
            flops=0, bytes_accessed=8 * units * unit * BLOCK, transcendentals=0
        ),
        name="weight_share",
    )(pos, item, block_weights)


def mixed_body(share, sizes, first, last, units, unit, order, pos_ref, item_ref, f_ref, w_ref, codes_ref, low_ref, *refs):
    steps = last - first
    far_refs, refs = refs[: 2 * steps], refs[2 * steps :]
    parts = len(order)
    far_w, refs = refs[:parts], refs[parts:]
    out_ref, f_buf, low_buf, far_buf, w_buf, out_buf, in_sems, w_sems, far_w_sems, out_sems = refs[-10:]
    dims = (((1,), (1,)), ((), ()))
    pieces = BLOCK // unit
    item = item_ref[0]
    starts = [sum(sizes[:one]) for one in range(len(sizes))]

    first_col, last_col = starts[first], starts[last - 1] + sizes[last - 1]
    gathered = []
    for way in range(2):
        for slot, apart in enumerate(order):
            for one in range(units):
                number = (item ^ apart) * units + one
                block, piece = lax.div(number, pieces), lax.rem(number, pieces)
                rows = pl.ds(pl.multiple_of(piece * unit, unit), unit)
                copy = pltpu.make_async_copy(
                    far_w[slot].at[way, one],
                    w_buf.at[2 + way, block, rows, :],
                    far_w_sems.at[way, number],
                )
                gathered.append(((block >= first_col) & (block < last_col), copy))
    loads = []
    for step in range(steps):
        chunk = first + step
        cols = pl.ds(starts[chunk] * BLOCK, sizes[chunk] * BLOCK)
        low_at, high_at = starts[chunk] // 2 * 2, (starts[chunk] + sizes[chunk] + 1) // 2 * 2
        both = pl.ds(low_at * BLOCK, (high_at - low_at) * BLOCK)
        copies = [
            pltpu.make_async_copy(f_ref.at[:, both], f_buf.at[:, both], in_sems.at[step, 0]),
            pltpu.make_async_copy(low_ref.at[:, cols], low_buf.at[:, cols], in_sems.at[step, 1]),
        ]
        for way in range(2):
            copies.append(
                pltpu.make_async_copy(
                    far_refs[way * steps + step], far_buf.at[way, :, cols], in_sems.at[step, 2 + way]
                )
            )
        for at in range(starts[chunk], starts[chunk] + sizes[chunk]):
            copies.append(
                pltpu.make_async_copy(w_ref.at[pos_ref[at]], w_buf.at[0, at], w_sems.at[0, at])
            )
            copies.append(
                pltpu.make_async_copy(
                    w_ref.at[pos_ref[share + (at ^ 1)]], w_buf.at[1, at], w_sems.at[1, at]
                )
            )
        loads.append(copies)
    for copy in loads[0]:
        copy.start()
    for wanted, copy in gathered:
        pl.when(wanted)(copy.start)
    for copies in loads[1:]:
        for copy in copies:
            copy.start()
    for way in range(2):
        for at in range(first_col, last_col):
            for piece in range(pieces):
                rows = pl.ds(piece * unit, unit)
                loads[[starts[one] <= at < starts[one] + sizes[one] for one in range(first, last)].index(True)].append(
                    pltpu.make_async_copy(
                        far_w[0].at[way, 0],
                        w_buf.at[2 + way, at, rows, :],
                        far_w_sems.at[way, at * pieces + piece],
                    )
                )
    stores = []
    for step in range(steps):
        chunk = first + step
        for copy in loads[step]:
            copy.wait()
        for at in range(starts[chunk], starts[chunk] + sizes[chunk]):
            own = slice(at * BLOCK, (at + 1) * BLOCK)
            flip = slice((at ^ 1) * BLOCK, ((at ^ 1) + 1) * BLOCK)
            total = lax.dot_general(f_buf[:, own], w_buf[0, at], dims, preferred_element_type=F32)
            total += lax.dot_general(f_buf[:, flip], w_buf[1, at], dims, preferred_element_type=F32)
            for way in range(2):
                total += lax.dot_general(
                    far_buf[way, :, own], w_buf[2 + way, at], dims, preferred_element_type=F32
                )
            total += jnp.dot(codes_ref[...], low_buf[:, own], preferred_element_type=F32)
            out_buf[:, own] = total.astype(BF16)
        cols = pl.ds(starts[chunk] * BLOCK, sizes[chunk] * BLOCK)
        store = pltpu.make_async_copy(out_buf.at[:, cols], out_ref.at[:, cols], out_sems.at[step])
        store.start()
        stores.append(store)
    for store in stores:
        store.wait()


def mixed_kernel(
    features, block_weights, codes, lowrank_out, far, far_weights, pos, item, sizes, first, last, units, order, held
):
    rows_here, width = features.shape
    share = width // BLOCK
    unit = far_weights[0].shape[2]
    hbm = pl.BlockSpec(memory_space=pltpu.HBM)
    smem = pl.BlockSpec(memory_space=pltpu.SMEM)
    far_inputs = [*far[0][first:last], *far[1][first:last], *far_weights]
    inputs = [pos, item, features, block_weights, codes, lowrank_out, *far_inputs]
    if held is not None:
        inputs.append(held)
    columns = sum(sizes[first:last])
    return pl.pallas_call(
        functools.partial(mixed_body, share, sizes, first, last, units, unit, order),
        in_specs=[smem, smem, hbm, hbm, pl.BlockSpec(memory_space=pltpu.VMEM), hbm]
        + [hbm] * (len(inputs) - 6),
        out_specs=hbm,
        out_shape=jax.ShapeDtypeStruct((rows_here, width), BF16),
        input_output_aliases={} if held is None else {len(inputs) - 1: 0},
        scratch_shapes=[
            pltpu.VMEM((rows_here, width), BF16),
            pltpu.VMEM(lowrank_out.shape, BF16),
            pltpu.VMEM((2, rows_here, width), BF16),
            pltpu.VMEM((4, share, BLOCK, BLOCK), BF16),
            pltpu.VMEM((rows_here, width), BF16),
            pltpu.SemaphoreType.DMA((last - first, 4)),
            pltpu.SemaphoreType.DMA((2, share)),
            pltpu.SemaphoreType.DMA((2, len(order) * units)),
            pltpu.SemaphoreType.DMA((last - first,)),
        ],
        compiler_params=pltpu.CompilerParams(vmem_limit_bytes=VMEM_LIMIT),
        cost_estimate=pl.CostEstimate(
            flops=9 * columns * rows_here * BLOCK * BLOCK,
            bytes_accessed=columns * BLOCK * 2 * (4 * rows_here + 4 * BLOCK),
            transcendentals=0,
        ),
        name="mixed",
    )(*inputs)


def place_body(keys, pairs, pos_ref, *refs):
    count = len(keys) * (2 if pairs else 1)
    inputs, refs = refs[:count], refs[-(count + 4) :]
    out_ref, bufs, (rows_ref, in_sems, out_sems) = refs[0], refs[1 : 1 + count], refs[1 + count :]
    loads = [
        pltpu.make_async_copy(inputs[one], bufs[one], in_sems.at[one]) for one in range(count)
    ]
    for copy in loads:
        copy.start()
    copies = []
    per = 2 if pairs else 1
    for one, numbers in enumerate(keys):
        for copy in loads[per * one : per * (one + 1)]:
            copy.wait()
        for at, key in enumerate(numbers):
            block = bufs[per * one][at].astype(F32)
            if pairs:
                block += bufs[per * one + 1][at].astype(F32)
            slot = len(copies)
            rows_ref[slot, :, 0, :] = block
            copy = pltpu.make_async_copy(
                rows_ref.at[slot], out_ref.at[:, pl.ds(pos_ref[key], 1), :], out_sems.at[slot]
            )
            copy.start()
            copies.append(copy)
    for copy in copies:
        copy.wait()


def place_kernel(pieces, keys, pos, held, stored, pairs=False):
    part = pieces[0].shape[1]
    total = sum(len(numbers) for numbers in keys)
    hbm = pl.BlockSpec(memory_space=pltpu.HBM)
    inputs = [pos, *pieces] + ([] if held is None else [held])
    return pl.pallas_call(
        functools.partial(place_body, keys, pairs),
        in_specs=[pl.BlockSpec(memory_space=pltpu.SMEM)] + [hbm] * (len(inputs) - 1),
        out_specs=hbm,
        out_shape=jax.ShapeDtypeStruct((part, stored, BLOCK), F32),
        input_output_aliases={} if held is None else {len(inputs) - 1: 0},
        scratch_shapes=[pltpu.VMEM(piece.shape, piece.dtype) for piece in pieces]
        + [
            pltpu.VMEM((total, part, 1, BLOCK), F32),
            pltpu.SemaphoreType.DMA((len(pieces),)),
            pltpu.SemaphoreType.DMA((total,)),
        ],
        compiler_params=pltpu.CompilerParams(vmem_limit_bytes=VMEM_LIMIT),
        cost_estimate=pl.CostEstimate(
            flops=0, bytes_accessed=8 * total * part * BLOCK, transcendentals=0
        ),
        name="place",
    )(*inputs)


def layer(features, cotangent, block_weights, block_rows, block_cols, lowrank_in, lowrank_out):
    _, width = features.shape
    share = width // BLOCK
    count = WIDTH // BLOCK
    stored = block_weights.shape[0]
    sizes = chunk_sizes(share)
    chunks = len(sizes)
    items = lax.axis_size("items")
    item = lax.axis_index("items").astype(jnp.int32)
    item_arg = item.reshape(1)
    groups = lax.axis_size("groups")
    sharer = (lax.axis_index("groups").astype(jnp.int32) * items + item).reshape(1)
    sharers = groups * items
    part = BLOCK // items
    bits = items.bit_length() - 1
    place = lax.axis_index("wloop")
    way_bits = lax.axis_size("wloop").bit_length() - 1
    far_bits = (way_bits - 2, way_bits - 1)

    def hop(value, bit):
        return swapped(value, "wloop", bit)

    stride_of = jnp.bitwise_xor(block_rows, block_cols)
    stride_id = (stride_of == 1) * 1 + (stride_of == count // 4) * 2 + (stride_of == count // 2) * 3
    key = stride_id * share + block_cols % share
    pos = jnp.sum(
        jnp.where(
            key[None, :] == jnp.arange(4 * share, dtype=jnp.int32)[:, None],
            jnp.arange(stored, dtype=jnp.int32)[None, :],
            0,
        ),
        axis=1,
    ).astype(jnp.int32)

    far, source = [[], []], features
    for one in range(chunks):
        first = sum(sizes[:one]) * BLOCK
        piece = source[:, first : first + sizes[one] * BLOCK]
        if one + 1 < chunks:
            source = after(source, piece)
        for way in range(2):
            far[way].append(hop(piece, far_bits[way]))

    unit = min(BLOCK, share * BLOCK // sharers)
    units = share * BLOCK // sharers // unit
    shares = weight_share(block_weights, pos, sharer, share, unit, units)
    held = [hop(shares[way], far_bits[way]) for way in range(2)]
    far_weights, order = [jnp.stack(held)], [0]
    hops = [("items", level, 1 << level) for level in range(bits - 1, 0, -1)]
    hops += [("groups", level, items << level) for level in range(groups.bit_length() - 1)]
    hops += [("items", 0, 1)]
    for axis, level, apart in hops:
        for one in range(len(order)):
            far_weights.append(swapped(far_weights[one], axis, level))
            order.append(order[one] ^ apart)

    dims = (((1,), (1,)), ((), ()))
    codes = jnp.stack(
        [
            lax.dot_general(features, lowrank_in, dims, preferred_element_type=F32),
            lax.dot_general(cotangent, lowrank_out, dims, preferred_element_type=F32),
        ]
    )
    for level in range(way_bits - 1):
        mine = (place >> level) & 1
        split = codes.reshape(2, 2, codes.shape[1] // 2, codes.shape[2])
        codes = pick(split, mine, 1) + hop(pick(split, 1 - mine, 1), level)
    came = hop(codes, way_bits - 1)
    codes = (codes + came).astype(BF16)
    for level in range(way_bits - 2, -1, -1):
        mine = (place >> level) & 1
        other = hop(codes, level)
        codes = jnp.where(
            mine == 0,
            jnp.concatenate([codes, other], axis=1),
            jnp.concatenate([other, codes], axis=1),
        )
    codes, backs = codes[0], codes[1]

    bit = item_arg & 1
    own = pair_grads(bit, cotangent, [features], ((0, 0), (0, 1)), 0, share, items)
    own = items_sum(*own, item)
    shape = (2 * share, part, BLOCK)
    block_grads = place_kernel(
        [own[0].reshape(shape), own[1].reshape(shape)],
        [list(range(2 * share))],
        pos,
        None,
        stored,
        pairs=True,
    )
    returned = [[], []]
    for one in range(chunks):
        pairs = pair_grads(
            bit,
            cotangent,
            [far[0][one], far[1][one]],
            ((0, 0), (1, 0)),
            sum(sizes[:one]),
            sizes[one],
            items,
        )
        keep, came = items_sum(*pairs, item)
        for way in range(2):
            done = (keep[way] + came[way].astype(F32)).astype(BF16)
            returned[way].append(hop(done, far_bits[way]))

    low = low_kernel(bit, backs, features, codes, cotangent, items)
    keep, came = items_sum(*low, item)
    low = [keep[way] + came[way].astype(F32) for way in range(2)]

    mixed = None
    cuts = [0, *range(max(1, chunks - 2), chunks + 1)]
    for first, last in zip(cuts, cuts[1:]):
        mixed = mixed_kernel(
            features,
            block_weights,
            codes,
            lowrank_out,
            far,
            far_weights,
            pos,
            sharer,
            sizes,
            first,
            last,
            units,
            order,
            mixed,
        )
    for first, last in ((0, chunks - 1), (chunks - 1, chunks)):
        pieces, keys = [], []
        for way in range(2):
            for one in range(first, last):
                start = (2 + way) * share + sum(sizes[:one])
                pieces.append(returned[way][one])
                keys.append(list(range(start, start + sizes[one])))
        block_grads = place_kernel(pieces, keys, pos, block_grads, stored)
    return (mixed, block_grads, low[0], low[1])


def chunk_sizes(share):
    return CHUNK_SIZES if sum(CHUNK_SIZES) == share else (1,) * share


def solution(mesh):
    return jax.shard_map(
        layer,
        mesh=mesh,
        in_specs=(
            P(("groups", "items"), "wloop"),
            P(("groups", "items"), "wloop"),
            P("wloop", None, None),
            P("wloop"),
            P("wloop"),
            P(None, "wloop"),
            P(None, "wloop"),
        ),
        out_specs=(
            P(("groups", "items"), "wloop"),
            P(("groups", "items"), "wloop", None),
            P(("groups", "items"), "wloop"),
            P(("groups", "items"), "wloop"),
        ),
        check_vma=False,
    )
```

```python
import functools

import jax
import jax.numpy as jnp
from jax import lax
from jax.experimental import pallas as pl
from jax.experimental.pallas import tpu as pltpu
from jax.sharding import PartitionSpec as P


WIDTH = 16384
BLOCK = 256
VMEM_LIMIT = 67_043_328
CHUNK_SIZES = (4, 4, 5, 3)


F32 = jnp.float32
BF16 = jnp.bfloat16


def swapped(block, axis, apart):
    count = lax.axis_size(axis)
    return lax.ppermute(block, axis, [(one, one ^ (1 << apart)) for one in range(count)])


def after(value, *deps):
    return lax.optimization_barrier((value, *deps))[0]


def pick(values, index, dim):
    return lax.dynamic_index_in_dim(values, index, dim, keepdims=False)


def grad_body(pairs, part, first, step, bit_ref, g_ref, *refs):
    count = (len(refs) - 7) // 2
    f_refs, (send_ref, keep_ref, g_buf), refs = refs[:count], refs[count : count + 3], refs[count + 3 :]
    f_bufs, (send_buf, keep_buf, in_sems, out_sems) = refs[:count], refs[count:]
    bit = bit_ref[0]
    groups = g_buf.shape[1] // (step * BLOCK)
    halves = send_ref.shape[0]
    loads = []
    for group in range(groups):
        cols = pl.ds(group * step * BLOCK, step * BLOCK)
        there = pl.ds((first + group * step) * BLOCK, step * BLOCK)
        loads.append(
            [pltpu.make_async_copy(g_ref.at[:, there], g_buf.at[:, cols], in_sems.at[group, 0])]
            + [
                pltpu.make_async_copy(
                    f_refs[one].at[:, cols], f_bufs[one].at[:, cols], in_sems.at[group, 1 + one]
                )
                for one in range(count)
            ]
        )
    for copies in loads:
        for copy in copies:
            copy.start()
    stores = []
    for group in range(groups):
        for copy in loads[group]:
            copy.wait()
        for at in range(group * step, (group + 1) * step):
            for slot, (f_at, flip) in enumerate(pairs):
                g_at = at ^ flip
                total = lax.dot_general(
                    g_buf[:, g_at * BLOCK : (g_at + 1) * BLOCK],
                    f_bufs[f_at][:, at * BLOCK : (at + 1) * BLOCK],
                    (((0,), (0,)), ((), ())),
                    preferred_element_type=F32,
                )
                for half in range(halves):
                    low = total[2 * half * part : (2 * half + 1) * part]
                    high = total[(2 * half + 1) * part : (2 * half + 2) * part]
                    keep_buf[half, slot, at] = jnp.where(bit == 0, low, high)
                    send_buf[half, slot, at] = jnp.where(bit == 0, high, low).astype(BF16)
        span = pl.ds(group * step, step)
        for which, (buf, ref) in enumerate(((send_buf, send_ref), (keep_buf, keep_ref))):
            copy = pltpu.make_async_copy(
                buf.at[:, :, span], ref.at[:, :, span], out_sems.at[group, which]
            )
            copy.start()
            stores.append(copy)
    for copy in stores:
        copy.wait()


def pair_grads(bit, cotangent, features, pairs, first, count, parts):
    rows_here = cotangent.shape[0]
    part = BLOCK // parts
    step = 2 if count % 2 == 0 else 1
    shape = (parts // 2, 2, count, part, BLOCK)
    wide = pltpu.VMEM((rows_here, count * BLOCK), BF16)
    hbm = pl.BlockSpec(memory_space=pltpu.HBM)
    return pl.pallas_call(
        functools.partial(grad_body, pairs, part, first, step),
        in_specs=[pl.BlockSpec(memory_space=pltpu.SMEM)] + [hbm] * (1 + len(features)),
        out_specs=(hbm, hbm),
        scratch_shapes=[wide] * (1 + len(features))
        + [
            pltpu.VMEM(shape, BF16),
            pltpu.VMEM(shape, F32),
            pltpu.SemaphoreType.DMA((count // step, 1 + len(features))),
            pltpu.SemaphoreType.DMA((count // step, 2)),
        ],
        out_shape=(jax.ShapeDtypeStruct(shape, BF16), jax.ShapeDtypeStruct(shape, F32)),
        compiler_params=pltpu.CompilerParams(vmem_limit_bytes=VMEM_LIMIT),
        cost_estimate=pl.CostEstimate(
            flops=4 * count * rows_here * BLOCK * BLOCK,
            bytes_accessed=count * BLOCK * (2 * rows_here * 3 + 6 * BLOCK),
            transcendentals=0,
        ),
        name="pair_grads",
    )(bit, cotangent, *features)


def low_body(part, step, bit_ref, b_ref, f_ref, c_ref, g_ref, send_ref, keep_ref, *refs):
    f_buf, g_buf, send_buf, keep_buf, in_sems, out_sems = refs
    bit = bit_ref[0]
    groups = f_buf.shape[1] // step
    loads, stores = [], []
    for group in range(groups):
        cols = pl.ds(group * step, step)
        loads.append(
            [
                pltpu.make_async_copy(ref.at[:, cols], buf.at[:, cols], in_sems.at[group, one])
                for one, (ref, buf) in enumerate(((f_ref, f_buf), (g_ref, g_buf)))
            ]
        )
    for copies in loads:
        for copy in copies:
            copy.start()
    for group in range(groups):
        cols = slice(group * step, (group + 1) * step)
        for slot, (small, wide) in enumerate(((b_ref, f_buf), (c_ref, g_buf))):
            loads[group][slot].wait()
            total = lax.dot_general(
                small[...], wide[:, cols], (((0,), (0,)), ((), ())), preferred_element_type=F32
            )
            for half in range(send_ref.shape[0]):
                low = total[2 * half * part : (2 * half + 1) * part]
                high = total[(2 * half + 1) * part : (2 * half + 2) * part]
                keep_buf[half, slot, :, cols] = jnp.where(bit == 0, low, high)
                send_buf[half, slot, :, cols] = jnp.where(bit == 0, high, low).astype(BF16)
        span = pl.ds(group * step, step)
        for which, (buf, ref) in enumerate(((send_buf, send_ref), (keep_buf, keep_ref))):
            copy = pltpu.make_async_copy(
                buf.at[:, :, :, span], ref.at[:, :, :, span], out_sems.at[group, which]
            )
            copy.start()
            stores.append(copy)
    for copy in stores:
        copy.wait()


def low_kernel(bit, backs, features, codes, cotangent, parts):
    rows_here, width = features.shape
    rank = codes.shape[1]
    part = rank // parts
    step = min(1024, width)
    shape = (parts // 2, 2, part, width)
    hbm, vmem = pl.BlockSpec(memory_space=pltpu.HBM), pl.BlockSpec(memory_space=pltpu.VMEM)
    return pl.pallas_call(
        functools.partial(low_body, part, step),
        in_specs=[pl.BlockSpec(memory_space=pltpu.SMEM), vmem, hbm, vmem, hbm],
        out_specs=(hbm, hbm),
        scratch_shapes=[
            pltpu.VMEM((rows_here, width), BF16),
            pltpu.VMEM((rows_here, width), BF16),
            pltpu.VMEM(shape, BF16),
            pltpu.VMEM(shape, F32),
            pltpu.SemaphoreType.DMA((width // step, 2)),
            pltpu.SemaphoreType.DMA((width // step, 2)),
        ],
        out_shape=(jax.ShapeDtypeStruct(shape, BF16), jax.ShapeDtypeStruct(shape, F32)),
        compiler_params=pltpu.CompilerParams(vmem_limit_bytes=VMEM_LIMIT),
        cost_estimate=pl.CostEstimate(
            flops=4 * rank * rows_here * width,
            bytes_accessed=width * (4 * rows_here + 6 * rank),
            transcendentals=0,
        ),
        name="low_grads",
    )(bit, backs, features, codes, cotangent)


def items_sum(send, keep, index):
    bits = lax.axis_size("items").bit_length() - 1
    came = swapped(send, "items", 0)
    for level in range(1, bits):
        mine = (index >> level) & 1
        shape = (keep.shape[0] // 2, 2, *keep.shape[1:])
        keep, came = keep.reshape(shape), came.reshape(shape)
        leave = pick(keep, 1 - mine, 1) + pick(came, 1 - mine, 1).astype(F32)
        keep = pick(keep, mine, 1) + pick(came, mine, 1).astype(F32)
        came = swapped(leave.astype(BF16), "items", level)
    return keep[0], came[0]


def share_body(share, units, unit, pos_ref, item_ref, w_ref, *refs):
    out_refs, sems = refs[:2], refs[2]
    pieces = BLOCK // unit
    copies = []
    for way in range(2):
        for one in range(units):
            number = item_ref[0] * units + one
            block = pos_ref[(2 + way) * share + lax.div(number, pieces)]
            first = pl.multiple_of(lax.rem(number, pieces) * unit, unit)
            copies.append(
                pltpu.make_async_copy(
                    w_ref.at[block, pl.ds(first, unit), :],
                    out_refs[way].at[one],
                    sems.at[way * units + one],
                )
            )
    for copy in copies:
        copy.start()
    for copy in copies:
        copy.wait()


def weight_share(block_weights, pos, item, share, unit, units):
    return pl.pallas_call(
        functools.partial(share_body, share, units, unit),
        in_specs=[
            pl.BlockSpec(memory_space=pltpu.SMEM),
            pl.BlockSpec(memory_space=pltpu.SMEM),
            pl.BlockSpec(memory_space=pl.ANY),
        ],
        out_specs=(pl.BlockSpec(memory_space=pltpu.VMEM),) * 2,
        out_shape=(jax.ShapeDtypeStruct((units, unit, BLOCK), BF16),) * 2,
        scratch_shapes=[pltpu.SemaphoreType.DMA((2 * units,))],
        compiler_params=pltpu.CompilerParams(vmem_limit_bytes=VMEM_LIMIT),
        cost_estimate=pl.CostEstimate(
            flops=0, bytes_accessed=8 * units * unit * BLOCK, transcendentals=0
        ),
        name="weight_share",
    )(pos, item, block_weights)


def mixed_body(share, sizes, first, last, units, unit, order, pos_ref, item_ref, f_ref, w_ref, codes_ref, low_ref, *refs):
    steps = last - first
    far_refs, refs = refs[: 2 * steps], refs[2 * steps :]
    parts = len(order)
    far_w, refs = refs[:parts], refs[parts:]
    out_ref, f_buf, low_buf, far_buf, w_buf, out_buf, in_sems, w_sems, far_w_sems, out_sems = refs[-10:]
    dims = (((1,), (1,)), ((), ()))
    pieces = BLOCK // unit
    item = item_ref[0]
    starts = [sum(sizes[:one]) for one in range(len(sizes))]

    first_col, last_col = starts[first], starts[last - 1] + sizes[last - 1]
    gathered = []
    for way in range(2):
        for slot, apart in enumerate(order):
            owner = item ^ apart
            source = far_w[slot].at[way]
            if pieces == 1:
                block, after_block = owner * units, owner * units + units
                into = w_buf.at[2 + way, pl.ds(block, units)]
            else:
                block = lax.div(owner, pieces)
                after_block = block + 1
                rows = pl.ds(pl.multiple_of(lax.rem(owner, pieces) * unit, unit), unit)
                into = w_buf.at[2 + way, pl.ds(block, 1), rows, :]
            copy = pltpu.make_async_copy(source, into, far_w_sems.at[way, owner])
            gathered.append(((after_block > first_col) & (block < last_col), copy))
    loads = []
    for step in range(steps):
        chunk = first + step
        cols = pl.ds(starts[chunk] * BLOCK, sizes[chunk] * BLOCK)
        low_at, high_at = starts[chunk] // 2 * 2, (starts[chunk] + sizes[chunk] + 1) // 2 * 2
        both = pl.ds(low_at * BLOCK, (high_at - low_at) * BLOCK)
        copies = [
            pltpu.make_async_copy(f_ref.at[:, both], f_buf.at[:, both], in_sems.at[step, 0]),
            pltpu.make_async_copy(low_ref.at[:, cols], low_buf.at[:, cols], in_sems.at[step, 1]),
        ]
        for way in range(2):
            copies.append(
                pltpu.make_async_copy(
                    far_refs[way * steps + step], far_buf.at[way, :, cols], in_sems.at[step, 2 + way]
                )
            )
        for at in range(starts[chunk], starts[chunk] + sizes[chunk]):
            copies.append(
                pltpu.make_async_copy(w_ref.at[pos_ref[at]], w_buf.at[0, at], w_sems.at[0, at])
            )
            copies.append(
                pltpu.make_async_copy(
                    w_ref.at[pos_ref[share + (at ^ 1)]], w_buf.at[1, at], w_sems.at[1, at]
                )
            )
        loads.append(copies)
    for copy in loads[0]:
        copy.start()
    for wanted, copy in gathered:
        pl.when(wanted)(copy.start)
    for copies in loads[1:]:
        for copy in copies:
            copy.start()
    for way in range(2):
        for owner in range(first_col * pieces // units, -(-last_col * pieces // units)):
            block = max(owner * units // pieces, first_col)
            rows = pl.ds(owner % pieces * unit, unit)
            into = w_buf.at[2 + way, pl.ds(owner * units // pieces, units), rows, :]
            copy = pltpu.make_async_copy(far_w[0].at[way], into, far_w_sems.at[way, owner])
            step = [starts[one] <= block < starts[one] + sizes[one] for one in range(first, last)]
            loads[step.index(True)].append(copy)
    stores = []
    for step in range(steps):
        chunk = first + step
        for copy in loads[step]:
            copy.wait()
        for at in range(starts[chunk], starts[chunk] + sizes[chunk]):
            own = slice(at * BLOCK, (at + 1) * BLOCK)
            flip = slice((at ^ 1) * BLOCK, ((at ^ 1) + 1) * BLOCK)
            total = lax.dot_general(f_buf[:, own], w_buf[0, at], dims, preferred_element_type=F32)
            total += lax.dot_general(f_buf[:, flip], w_buf[1, at], dims, preferred_element_type=F32)
            for way in range(2):
                total += lax.dot_general(
                    far_buf[way, :, own], w_buf[2 + way, at], dims, preferred_element_type=F32
                )
            total += jnp.dot(codes_ref[...], low_buf[:, own], preferred_element_type=F32)
            out_buf[:, own] = total.astype(BF16)
        cols = pl.ds(starts[chunk] * BLOCK, sizes[chunk] * BLOCK)
        store = pltpu.make_async_copy(out_buf.at[:, cols], out_ref.at[:, cols], out_sems.at[step])
        store.start()
        stores.append(store)
    for store in stores:
        store.wait()


def mixed_kernel(
    features, block_weights, codes, lowrank_out, far, far_weights, pos, item, sizes, first, last, units, order, held
):
    rows_here, width = features.shape
    share = width // BLOCK
    unit = far_weights[0].shape[2]
    hbm = pl.BlockSpec(memory_space=pltpu.HBM)
    smem = pl.BlockSpec(memory_space=pltpu.SMEM)
    far_inputs = [*far[0][first:last], *far[1][first:last], *far_weights]
    inputs = [pos, item, features, block_weights, codes, lowrank_out, *far_inputs]
    if held is not None:
        inputs.append(held)
    columns = sum(sizes[first:last])
    return pl.pallas_call(
        functools.partial(mixed_body, share, sizes, first, last, units, unit, order),
        in_specs=[smem, smem, hbm, hbm, pl.BlockSpec(memory_space=pltpu.VMEM), hbm]
        + [hbm] * (len(inputs) - 6),
        out_specs=hbm,
        out_shape=jax.ShapeDtypeStruct((rows_here, width), BF16),
        input_output_aliases={} if held is None else {len(inputs) - 1: 0},
        scratch_shapes=[
            pltpu.VMEM((rows_here, width), BF16),
            pltpu.VMEM(lowrank_out.shape, BF16),
            pltpu.VMEM((2, rows_here, width), BF16),
            pltpu.VMEM((4, share, BLOCK, BLOCK), BF16),
            pltpu.VMEM((rows_here, width), BF16),
            pltpu.SemaphoreType.DMA((last - first, 4)),
            pltpu.SemaphoreType.DMA((2, share)),
            pltpu.SemaphoreType.DMA((2, len(order))),
            pltpu.SemaphoreType.DMA((last - first,)),
        ],
        compiler_params=pltpu.CompilerParams(vmem_limit_bytes=VMEM_LIMIT),
        cost_estimate=pl.CostEstimate(
            flops=9 * columns * rows_here * BLOCK * BLOCK,
            bytes_accessed=columns * BLOCK * 2 * (4 * rows_here + 4 * BLOCK),
            transcendentals=0,
        ),
        name="mixed",
    )(*inputs)


def place_body(keys, pairs, pos_ref, *refs):
    count = len(keys) * (2 if pairs else 1)
    inputs, refs = refs[:count], refs[-(count + 4) :]
    out_ref, bufs, (rows_ref, in_sems, out_sems) = refs[0], refs[1 : 1 + count], refs[1 + count :]
    loads = [
        pltpu.make_async_copy(inputs[one], bufs[one], in_sems.at[one]) for one in range(count)
    ]
    for copy in loads:
        copy.start()
    copies = []
    per = 2 if pairs else 1
    for one, numbers in enumerate(keys):
        for copy in loads[per * one : per * (one + 1)]:
            copy.wait()
        for at, key in enumerate(numbers):
            block = bufs[per * one][at].astype(F32)
            if pairs:
                block += bufs[per * one + 1][at].astype(F32)
            slot = len(copies)
            rows_ref[slot, :, 0, :] = block
            copy = pltpu.make_async_copy(
                rows_ref.at[slot], out_ref.at[:, pl.ds(pos_ref[key], 1), :], out_sems.at[slot]
            )
            copy.start()
            copies.append(copy)
    for copy in copies:
        copy.wait()


def place_kernel(pieces, keys, pos, held, stored, pairs=False):
    part = pieces[0].shape[1]
    total = sum(len(numbers) for numbers in keys)
    hbm = pl.BlockSpec(memory_space=pltpu.HBM)
    inputs = [pos, *pieces] + ([] if held is None else [held])
    return pl.pallas_call(
        functools.partial(place_body, keys, pairs),
        in_specs=[pl.BlockSpec(memory_space=pltpu.SMEM)] + [hbm] * (len(inputs) - 1),
        out_specs=hbm,
        out_shape=jax.ShapeDtypeStruct((part, stored, BLOCK), F32),
        input_output_aliases={} if held is None else {len(inputs) - 1: 0},
        scratch_shapes=[pltpu.VMEM(piece.shape, piece.dtype) for piece in pieces]
        + [
            pltpu.VMEM((total, part, 1, BLOCK), F32),
            pltpu.SemaphoreType.DMA((len(pieces),)),
            pltpu.SemaphoreType.DMA((total,)),
        ],
        compiler_params=pltpu.CompilerParams(vmem_limit_bytes=VMEM_LIMIT),
        cost_estimate=pl.CostEstimate(
            flops=0, bytes_accessed=8 * total * part * BLOCK, transcendentals=0
        ),
        name="place",
    )(*inputs)


def layer(features, cotangent, block_weights, block_rows, block_cols, lowrank_in, lowrank_out):
    _, width = features.shape
    share = width // BLOCK
    count = WIDTH // BLOCK
    stored = block_weights.shape[0]
    sizes = chunk_sizes(share)
    chunks = len(sizes)
    items = lax.axis_size("items")
    item = lax.axis_index("items").astype(jnp.int32)
    item_arg = item.reshape(1)
    groups = lax.axis_size("groups")
    sharer = (lax.axis_index("groups").astype(jnp.int32) * items + item).reshape(1)
    sharers = groups * items
    part = BLOCK // items
    bits = items.bit_length() - 1
    place = lax.axis_index("wloop")
    way_bits = lax.axis_size("wloop").bit_length() - 1
    far_bits = (way_bits - 2, way_bits - 1)

    def hop(value, bit):
        return swapped(value, "wloop", bit)

    stride_of = jnp.bitwise_xor(block_rows, block_cols)
    stride_id = (stride_of == 1) * 1 + (stride_of == count // 4) * 2 + (stride_of == count // 2) * 3
    key = stride_id * share + block_cols % share
    pos = jnp.sum(
        jnp.where(
            key[None, :] == jnp.arange(4 * share, dtype=jnp.int32)[:, None],
            jnp.arange(stored, dtype=jnp.int32)[None, :],
            0,
        ),
        axis=1,
    ).astype(jnp.int32)

    far, source = [[], []], features
    for one in range(chunks):
        first = sum(sizes[:one]) * BLOCK
        piece = source[:, first : first + sizes[one] * BLOCK]
        if one + 1 < chunks:
            source = after(source, piece)
        for way in range(2):
            far[way].append(hop(piece, far_bits[way]))

    unit = min(BLOCK, share * BLOCK // sharers)
    units = share * BLOCK // sharers // unit
    shares = weight_share(block_weights, pos, sharer, share, unit, units)
    held = [hop(shares[way], far_bits[way]) for way in range(2)]
    far_weights, order = [jnp.stack(held)], [0]
    hops = [("items", level, 1 << level) for level in range(bits - 1, 0, -1)]
    hops += [("groups", level, items << level) for level in range(groups.bit_length() - 1)]
    hops += [("items", 0, 1)]
    for axis, level, apart in hops:
        for one in range(len(order)):
            far_weights.append(swapped(far_weights[one], axis, level))
            order.append(order[one] ^ apart)

    dims = (((1,), (1,)), ((), ()))
    codes = jnp.stack(
        [
            lax.dot_general(features, lowrank_in, dims, preferred_element_type=F32),
            lax.dot_general(cotangent, lowrank_out, dims, preferred_element_type=F32),
        ]
    )
    for level in range(way_bits - 1):
        mine = (place >> level) & 1
        split = codes.reshape(2, 2, codes.shape[1] // 2, codes.shape[2])
        codes = pick(split, mine, 1) + hop(pick(split, 1 - mine, 1), level)
    came = hop(codes, way_bits - 1)
    codes = (codes + came).astype(BF16)
    for level in range(way_bits - 2, -1, -1):
        mine = (place >> level) & 1
        other = hop(codes, level)
        codes = jnp.where(
            mine == 0,
            jnp.concatenate([codes, other], axis=1),
            jnp.concatenate([other, codes], axis=1),
        )
    codes, backs = codes[0], codes[1]

    bit = item_arg & 1
    own = pair_grads(bit, cotangent, [features], ((0, 0), (0, 1)), 0, share, items)
    own = items_sum(*own, item)
    shape = (2 * share, part, BLOCK)
    block_grads = place_kernel(
        [own[0].reshape(shape), own[1].reshape(shape)],
        [list(range(2 * share))],
        pos,
        None,
        stored,
        pairs=True,
    )
    returned = [[], []]
    for one in range(chunks):
        pairs = pair_grads(
            bit,
            cotangent,
            [far[0][one], far[1][one]],
            ((0, 0), (1, 0)),
            sum(sizes[:one]),
            sizes[one],
            items,
        )
        keep, came = items_sum(*pairs, item)
        for way in range(2):
            done = (keep[way] + came[way].astype(F32)).astype(BF16)
            returned[way].append(hop(done, far_bits[way]))

    low = low_kernel(bit, backs, features, codes, cotangent, items)
    keep, came = items_sum(*low, item)
    low = [keep[way] + came[way].astype(F32) for way in range(2)]

    mixed = None
    cuts = [0, max(1, chunks - 1), chunks]
    for first, last in zip(cuts, cuts[1:]):
        mixed = mixed_kernel(
            features,
            block_weights,
            codes,
            lowrank_out,
            far,
            far_weights,
            pos,
            sharer,
            sizes,
            first,
            last,
            units,
            order,
            mixed,
        )
    for first, last in ((0, chunks - 1), (chunks - 1, chunks)):
        pieces, keys = [], []
        for way in range(2):
            for one in range(first, last):
                start = (2 + way) * share + sum(sizes[:one])
                pieces.append(returned[way][one])
                keys.append(list(range(start, start + sizes[one])))
        block_grads = place_kernel(pieces, keys, pos, block_grads, stored)
    return (mixed, block_grads, low[0], low[1])


def chunk_sizes(share):
    return CHUNK_SIZES if sum(CHUNK_SIZES) == share else (1,) * share


def solution(mesh):
    return jax.shard_map(
        layer,
        mesh=mesh,
        in_specs=(
            P(("groups", "items"), "wloop"),
            P(("groups", "items"), "wloop"),
            P("wloop", None, None),
            P("wloop"),
            P("wloop"),
            P(None, "wloop"),
            P(None, "wloop"),
        ),
        out_specs=(
            P(("groups", "items"), "wloop"),
            P(("groups", "items"), "wloop", None),
            P(("groups", "items"), "wloop"),
            P(("groups", "items"), "wloop"),
        ),
        check_vma=False,
    )
```
